32 devices in a mesh: band: 4 (over y, core), shard: 8 (over z, x).
Axes of the slice: x: 2, y: 2, z: 4, core: 2. Of those that a mesh axis runs over, the one named last changes fastest.
Arguments:
- block_input: bfloat16 [8, 56, 14, 512], P('shard', 'band'), may hold values from -6 to 6
- output_grad: bfloat16 [8, 56, 14, 512], P('shard', 'band'), may hold values from -6 to 6
- region_ids: int32 [56, 14], P('band'), may hold values from 0 to 8, as said below
- relative_index: int32 [49, 49], replicated, may hold values from 0 to 168
- attention_weight: float32 [512, 2048], P('shard'), may hold values from -0.375 to 0.375
- expand_weight: float32 [512, 2048], P('shard'), may hold values from -0.25 to 0.25
- reduce_weight: float32 [2048, 512], P('shard'), may hold values from -0.125 to 0.125
- vectors: float32 [12, 512], P(None, 'shard'), may hold values from -0.5 to 0.5
- bias_table: float32 [169, 16], replicated, may hold values from -0.6 to 250
- attention_mean: float32 [512, 2048], P('shard'), may hold values from -0.3 to 0.3
- attention_square: float32 [512, 2048], P('shard'), may hold values from 0.0001 to 0.001
- expand_mean: float32 [512, 2048], P('shard'), may hold values from -0.3 to 0.3
- expand_square: float32 [512, 2048], P('shard'), may hold values from 0.0001 to 0.001
- reduce_mean: float32 [2048, 512], P('shard'), may hold values from -0.3 to 0.3
- reduce_square: float32 [2048, 512], P('shard'), may hold values from 0.0001 to 0.001
- vectors_mean: float32 [12, 512], P(None, 'shard'), may hold values from -0.3 to 0.3
- vectors_square: float32 [12, 512], P(None, 'shard'), may hold values from 0.0001 to 0.001
- table_mean: float32 [169, 16], replicated, may hold values from -0.3 to 0.3
- table_square: float32 [169, 16], replicated, may hold values from 0.0001 to 0.001
Outputs:
- block_output: float32 [8, 56, 14, 512], P('shard', 'band')
- input_grad: float32 [8, 56, 14, 512], P('shard', 'band')
- attention_grad: float32 [512, 2048], P('shard')
- expand_grad: float32 [512, 2048], P('shard')
- reduce_grad: float32 [2048, 512], P('shard')
- vectors_grad: float32 [12, 512], P(None, 'shard')
- table_grad: float32 [169, 16], replicated
- new_attention: float32 [512, 2048], P('shard')
- new_expand: float32 [512, 2048], P('shard')
- new_reduce: float32 [2048, 512], P('shard')
- new_vectors: float32 [12, 512], P(None, 'shard')
- new_table: float32 [169, 16], replicated
- new_attention_mean: float32 [512, 2048], P('shard')
- new_attention_square: float32 [512, 2048], P('shard')
- new_expand_mean: float32 [512, 2048], P('shard')
- new_expand_square: float32 [512, 2048], P('shard')
- new_reduce_mean: float32 [2048, 512], P('shard')
- new_reduce_square: float32 [2048, 512], P('shard')
- new_vectors_mean: float32 [12, 512], P(None, 'shard')
- new_vectors_square: float32 [12, 512], P(None, 'shard')
- new_table_mean: float32 [169, 16], replicated
- new_table_square: float32 [169, 16], replicated
The draws below stay inside these ranges and needn't reach their ends.
Inputs may be any that keep to these rules, and one draw needn't show every extreme that they name: region_ids[r, c] = 3 * a(r) + b(c), where a(r) is 0 for r < 49, 1 from there up to a cut inside the last 7 rows, 2 from the cut on; b(c) likewise over the 14 columns with a cut of its own; each cut leaves 1 to 6 tokens in region 2.
All inputs are finite; a program needn't handle non-finite values.
Results may differ from the reference program's by a relative error of at most 0.023.
Values may be sent and summed in bfloat16 or wider, within the bound.
A program may use at most 128 MiB of HBM per device.

```python
import math
import jax
import jax.numpy as jnp
from jax import lax

C = 512
HEADS = 16
FFN = 2048
WIN = 7
SHIFT = 3
STEP = 5
H = 56
W = 14
IMAGES = 8
WTOK = 49
TABLE = 169


def draw_region_ids(key, part):
    row_key = jax.random.fold_in(key, 11)
    col_key = jax.random.fold_in(key, 13)
    row_cut = jax.random.randint(row_key, (), 1, WIN)
    col_cut = jax.random.randint(col_key, (), 1, WIN)
    rows = jnp.arange(H, dtype=jnp.int32)
    cols = jnp.arange(W, dtype=jnp.int32)
    row_region = (rows >= H - WIN).astype(jnp.int32) + (rows >= H - row_cut).astype(jnp.int32)
    col_region = (cols >= W - WIN).astype(jnp.int32) + (cols >= W - col_cut).astype(jnp.int32)
    return 3 * row_region[:, None] + col_region[None, :]


def draw_bias_table(key, part):
    base_key = jax.random.fold_in(key, 0)
    table_draw = jnp.clip(0.15 * jax.random.normal(base_key, (TABLE, HEADS), jnp.float32), -0.6, 0.6)
    return table_draw


def with_ends(values, own_key, smallest, high):
    extent = values.shape
    place = [jax.random.randint(jax.random.fold_in(own_key, axis), (), 0, extent[axis]) for axis in range(len(extent))]
    values = values.at[tuple(place)].set(smallest)
    longest = extent.index(max(extent))
    place[longest] = (place[longest] + 1) % extent[longest]
    return values.at[tuple(place)].set(high)


def with_spikes(array, rng, source, target, blocks, factor):
    owner, partner = [(jnp.arange(array.shape[dim]) // (array.shape[dim] // blocks)).reshape([-1 if axis == dim else 1 for axis in range(array.ndim)]) for dim in (source, target)]
    chosen = jax.random.permutation(rng, blocks)[partner]
    strong = (owner == chosen) | (owner == (partner + blocks // 2) % blocks)
    return jnp.where(strong, factor * array, array)


def level_of(stream_key, extent, pieces, low, high):
    def one(position, blocks):
        draws = jax.random.uniform(jax.random.fold_in(jax.random.fold_in(stream_key, 6), position), (blocks,), jnp.float32, low / len(pieces), high / len(pieces))
        return jnp.repeat(jnp.exp(draws), extent[position] // blocks).reshape((-1,) + (1,) * (len(extent) - position - 1))

    level = one(*pieces[0])
    for cut in pieces[1:]:
        level = level * one(*cut)
    return level


def bell_draw(stream_key, extent, deviation, most, cuts=(), held_as=jnp.bfloat16):
    result = jax.random.normal(stream_key, extent, jnp.float32) * deviation
    if len(cuts) > 0:
        result = level_of(stream_key, extent, cuts, -0.22, 0.18) * result
    return jnp.clip(result, min=-most, max=most).astype(held_as)


def heavy_noise(stream_key, dims, spread, bound, pieces, heavy, kind=jnp.bfloat16):
    array = spread * jax.random.normal(stream_key, dims, jnp.float32)
    if pieces:
        array = array * level_of(stream_key, dims, pieces, -0.22, 0.18)
    return jnp.clip(with_spikes(array, jax.random.fold_in(stream_key, 3), *heavy), -bound, bound).astype(kind)


def setup_inputs(seed: int = 0) -> dict:
    streams_of = jax.random.split(jax.random.key(seed), 20)
    return {
        "block_input": bell_draw(streams_of[0], (IMAGES, H, W, C), 1.0, 6.0, ((0, 8), (1, 4))),
        "output_grad": heavy_noise(streams_of[1], (IMAGES, H, W, C), 1.0, 6.0, ((0, 8), (1, 4)), (0, 3, 8, 2.0)),
        "region_ids": draw_region_ids(jax.random.fold_in(streams_of[19], 71), 0),
        "relative_index": with_ends(jax.random.randint(streams_of[3], (WTOK, WTOK), 0, TABLE), jax.random.fold_in(streams_of[3], 1), 0, TABLE - 1).astype(jnp.int32),
        "attention_weight": bell_draw(streams_of[4], (C, 4 * C), (C // 2) ** -0.5, 0.375, ((0, 8),), jnp.float32),
        "expand_weight": bell_draw(streams_of[5], (C, FFN), C ** -0.5, 0.25, ((0, 8),), jnp.float32),
        "reduce_weight": bell_draw(streams_of[6], (FFN, C), FFN ** -0.5, 0.125, ((0, 8),), jnp.float32),
        "vectors": bell_draw(streams_of[7], (12, C), 0.1, 0.5, ((1, 8),), jnp.float32),
        "bias_table": draw_bias_table(jax.random.fold_in(streams_of[19], 71), 0),
        "attention_mean": bell_draw(streams_of[9], (C, 4 * C), 0.05, 0.3, ((0, 8),), jnp.float32),
        "attention_square": jnp.clip(jnp.exp(math.log(0.001) - 2.3025852 * jax.random.uniform(streams_of[10], (C, 4 * C), jnp.float32) ** level_of(streams_of[10], (C, 4 * C), ((0, 8),), -0.2, 0.2)), 0.0001, 0.001),
        "expand_mean": bell_draw(streams_of[11], (C, FFN), 0.05, 0.3, ((0, 8),), jnp.float32),
        "expand_square": jnp.clip(jnp.exp(math.log(0.001) - 2.3025852 * jax.random.uniform(streams_of[12], (C, FFN), jnp.float32) ** level_of(streams_of[12], (C, FFN), ((0, 8),), -0.2, 0.2)), 0.0001, 0.001),
        "reduce_mean": bell_draw(streams_of[13], (FFN, C), 0.05, 0.3, ((0, 8),), jnp.float32),
        "reduce_square": jnp.clip(jnp.exp(math.log(0.001) - 2.3025852 * jax.random.uniform(streams_of[14], (FFN, C), jnp.float32) ** level_of(streams_of[14], (FFN, C), ((0, 8),), -0.2, 0.2)), 0.0001, 0.001),
        "vectors_mean": bell_draw(streams_of[15], (12, C), 0.05, 0.3, ((1, 8),), jnp.float32),
        "vectors_square": jnp.clip(jnp.exp(math.log(0.001) - 2.3025852 * jax.random.uniform(streams_of[16], (12, C), jnp.float32) ** level_of(streams_of[16], (12, C), ((1, 8),), -0.2, 0.2)), 0.0001, 0.001),
        "table_mean": bell_draw(streams_of[17], (TABLE, HEADS), 0.05, 0.3, (), jnp.float32),
        "table_square": jnp.clip(jnp.exp(jax.random.uniform(streams_of[18], (TABLE, HEADS), jnp.float32, math.log(0.0001), math.log(0.001))), 0.0001, 0.001),
    }


NORM_EPS = 1e-05
LEARN_RATE = 0.02
BETA_ONE = 0.9
BETA_TWO = 0.999
ADAM_EPS = 1e-08
WEIGHT_DECAY = 0.05
MASK_VALUE = -1000000000.0

def to_windows(frame):
    image_count, rows_total, cols_total = (frame.shape[0], frame.shape[1], frame.shape[2])
    trailing = frame.shape[3:]
    blocks = frame.reshape((image_count, rows_total // WIN, WIN, cols_total // WIN, WIN) + trailing)
    blocks = jnp.moveaxis(blocks, 3, 2)
    return blocks.reshape((image_count * (rows_total // WIN) * (cols_total // WIN), WIN * WIN) + trailing)

def from_windows(blocks, image_count, rows_total, cols_total):
    trailing = blocks.shape[2:]
    frame = blocks.reshape((image_count, rows_total // WIN, cols_total // WIN, WIN, WIN) + trailing)
    frame = jnp.moveaxis(frame, 3, 2)
    return frame.reshape((image_count, rows_total, cols_total) + trailing)

def layer_normalize(values):
    center = lax.optimization_barrier(jnp.mean(values, axis=-1, keepdims=True))
    centered = values - center
    variance = lax.optimization_barrier(jnp.mean(centered * centered, axis=-1, keepdims=True))
    inverse_deviation = lax.rsqrt(variance + NORM_EPS)
    return (centered * inverse_deviation, inverse_deviation)

def normalize_backward(gradient_standardized, standardized_input, inverse_deviation):
    return inverse_deviation * (gradient_standardized - lax.optimization_barrier(jnp.mean(gradient_standardized, axis=-1, keepdims=True)) - standardized_input * lax.optimization_barrier(jnp.mean(gradient_standardized * standardized_input, axis=-1, keepdims=True)))

def gelu_parts(hidden_pre):
    normal_cdf = 0.5 * (1.0 + lax.erf(hidden_pre * (1.0 / math.sqrt(2.0))))
    density = jnp.exp(-0.5 * hidden_pre * hidden_pre) * (1.0 / math.sqrt(2.0 * math.pi))
    return (hidden_pre * normal_cdf, normal_cdf + hidden_pre * density)

def window_scores(per_head_queries, per_head_keys, same_region, pos_bias):
    raw = jnp.einsum('wihd,wjhd->whij', per_head_queries.astype(jnp.float32), per_head_keys.astype(jnp.float32))
    return jnp.where(same_region[:, None], raw + pos_bias[None], MASK_VALUE)

def forward(windows_in, same_region, matrices, row_vectors_list, pos_bias):
    attention, expand, shrink = matrices
    window_count, window_size, features = windows_in.shape
    head_count = pos_bias.shape[0]
    head_width = features // head_count
    score_scale = 1.0 / math.sqrt(head_width)
    incoming_tokens = windows_in.reshape(window_count * window_size, features).astype(jnp.float32)
    first_standardized, first_inverse_deviation = layer_normalize(incoming_tokens)
    first_normalized = (first_standardized * (1.0 + row_vectors_list[0]) + row_vectors_list[1]).astype(jnp.bfloat16)
    projected = jnp.dot(first_normalized, attention[:, :3 * features], preferred_element_type=jnp.float32)
    head_shape = (window_count, window_size, head_count, head_width)
    per_head_queries = ((projected[:, :features] + row_vectors_list[2]) * score_scale).astype(jnp.bfloat16).reshape(head_shape)
    per_head_keys = projected[:, features:2 * features].astype(jnp.bfloat16).reshape(head_shape)
    per_head_values = (projected[:, 2 * features:] + row_vectors_list[3]).astype(jnp.bfloat16).reshape(head_shape)
    scores = window_scores(per_head_queries, per_head_keys, same_region, pos_bias)
    row_peak = lax.optimization_barrier(jnp.max(scores, axis=-1, keepdims=True))
    powers = jnp.exp(scores - row_peak)
    totals = lax.optimization_barrier(jnp.sum(powers, axis=-1, keepdims=True))
    logarithm_total = row_peak + jnp.log(totals)
    prob_b = (powers / totals).astype(jnp.bfloat16)
    attended = jnp.einsum('whij,wjhd->wihd', prob_b.astype(jnp.float32), per_head_values.astype(jnp.float32))
    attended_bfloat = attended.reshape(window_count * window_size, features).astype(jnp.bfloat16)
    residual_stream = incoming_tokens + jnp.dot(attended_bfloat, attention[:, 3 * features:], preferred_element_type=jnp.float32) + row_vectors_list[4]
    second_standardized, second_inverse_deviation = layer_normalize(residual_stream)
    second_normalized = (second_standardized * (1.0 + row_vectors_list[5]) + row_vectors_list[6]).astype(jnp.bfloat16)
    hidden_pre = jnp.dot(second_normalized, expand, preferred_element_type=jnp.float32) + row_vectors_list[8:].reshape(-1)
    activated, gaussian_unit_slope = gelu_parts(hidden_pre)
    activated_bfloat = activated.astype(jnp.bfloat16)
    output = residual_stream + jnp.dot(activated_bfloat, shrink, preferred_element_type=jnp.float32) + row_vectors_list[7]
    stored_tensors = (first_standardized, first_inverse_deviation, first_normalized, per_head_queries, per_head_keys, per_head_values, logarithm_total, attended_bfloat, second_standardized, second_inverse_deviation, second_normalized, gaussian_unit_slope, activated_bfloat)
    return (output, stored_tensors)

def backward(stored_tensors, grad_windows, same_region, matrices, row_vectors_list, pos_bias):
    first_standardized, first_inverse_deviation, first_normalized, per_head_queries, per_head_keys, per_head_values, logarithm_total, attended_bfloat, second_standardized, second_inverse_deviation, second_normalized, gaussian_unit_slope, activated_bfloat = stored_tensors
    attention, expand, shrink = matrices
    window_count, window_size, head_count, head_width = per_head_queries.shape
    features = head_count * head_width
    score_scale = 1.0 / math.sqrt(head_width)
    rows_shape = (window_count * window_size, features)
    grad_rows = grad_windows.reshape(rows_shape)
    gradient_single_float = grad_rows.astype(jnp.float32)
    grad_obias = lax.optimization_barrier(jnp.sum(gradient_single_float, axis=0))
    grad_shrink = jnp.dot(activated_bfloat.T, grad_rows, preferred_element_type=jnp.float32)
    grad_act = jnp.dot(grad_rows, shrink.T, preferred_element_type=jnp.float32)
    grad_pre = grad_act * gaussian_unit_slope
    grad_pre_b = grad_pre.astype(jnp.bfloat16)
    grad_ebias = lax.optimization_barrier(jnp.sum(grad_pre, axis=0))
    grad_expand = jnp.dot(second_normalized.T, grad_pre_b, preferred_element_type=jnp.float32)
    gradient_second_normalized = jnp.dot(grad_pre_b, expand.T, preferred_element_type=jnp.float32)
    gradient_second_gain = lax.optimization_barrier(jnp.sum(gradient_second_normalized * second_standardized, axis=0))
    grad_beta_two = lax.optimization_barrier(jnp.sum(gradient_second_normalized, axis=0))
    gradient_residual_stream = gradient_single_float + normalize_backward(gradient_second_normalized * (1.0 + row_vectors_list[5]), second_standardized, second_inverse_deviation)
    grad_resid_b = gradient_residual_stream.astype(jnp.bfloat16)
    grad_pbias = lax.optimization_barrier(jnp.sum(gradient_residual_stream, axis=0))
    grad_outproj = jnp.dot(attended_bfloat.T, grad_resid_b, preferred_element_type=jnp.float32)
    head_shape = (window_count, window_size, head_count, head_width)
    grad_attended = jnp.dot(grad_resid_b, attention[:, 3 * features:].T, preferred_element_type=jnp.float32).astype(jnp.bfloat16).reshape(head_shape)
    scores = window_scores(per_head_queries, per_head_keys, same_region, pos_bias)
    prob_full = jnp.exp(scores - logarithm_total)
    prob_b = prob_full.astype(jnp.bfloat16)
    grad_probs = jnp.einsum('wihd,wjhd->whij', grad_attended.astype(jnp.float32), per_head_values.astype(jnp.float32))
    grad_value = jnp.einsum('whij,wihd->wjhd', prob_b.astype(jnp.float32), grad_attended.astype(jnp.float32))
    inner_sum = lax.optimization_barrier(jnp.sum(prob_full * grad_probs, axis=-1, keepdims=True))
    grad_scores = prob_full * (grad_probs - inner_sum)
    grad_posbias = lax.optimization_barrier(jnp.sum(grad_scores, axis=0))
    grad_scores_b = grad_scores.astype(jnp.bfloat16).astype(jnp.float32)
    grad_query = jnp.einsum('whij,wjhd->wihd', grad_scores_b, per_head_keys.astype(jnp.float32)) * score_scale
    grad_key = jnp.einsum('whij,wihd->wjhd', grad_scores_b, per_head_queries.astype(jnp.float32))
    grad_query = grad_query.reshape(rows_shape)
    grad_value = grad_value.reshape(rows_shape)
    grad_qkv = jnp.concatenate([grad_query, grad_key.reshape(rows_shape), grad_value], axis=1)
    grad_qkv_b = grad_qkv.astype(jnp.bfloat16)
    grad_inproj = jnp.dot(first_normalized.T, grad_qkv_b, preferred_element_type=jnp.float32)
    gradient_first_normalized = jnp.dot(grad_qkv_b, attention[:, :3 * features].T, preferred_element_type=jnp.float32)
    gradient_first_gain = lax.optimization_barrier(jnp.sum(gradient_first_normalized * first_standardized, axis=0))
    grad_beta_one = lax.optimization_barrier(jnp.sum(gradient_first_normalized, axis=0))
    gradient_token_rows = gradient_residual_stream + normalize_backward(gradient_first_normalized * (1.0 + row_vectors_list[0]), first_standardized, first_inverse_deviation)
    grad_attention = jnp.concatenate([grad_inproj, grad_outproj], axis=1)
    grad_vectors = jnp.concatenate([jnp.stack([gradient_first_gain, grad_beta_one, lax.optimization_barrier(jnp.sum(grad_query, axis=0)), lax.optimization_barrier(jnp.sum(grad_value, axis=0)), grad_pbias, gradient_second_gain, grad_beta_two, grad_obias]), grad_ebias.reshape(4, features)], axis=0)
    return (gradient_token_rows, (grad_attention, grad_expand, grad_shrink, grad_vectors, grad_posbias))

def adamw(weight, grad, first, second, decay):
    first_new = BETA_ONE * first + (1.0 - BETA_ONE) * grad
    second_new = BETA_TWO * second + (1.0 - BETA_TWO) * grad * grad
    corr_one = 1.0 - BETA_ONE ** STEP
    corr_two = 1.0 - BETA_TWO ** STEP
    step_dir = first_new / corr_one / (jnp.sqrt(second_new / corr_two) + ADAM_EPS)
    return (weight - LEARN_RATE * (step_dir + decay * weight), first_new, second_new)

def reference(block_input, output_grad, region_ids, relative_index, attention_weight, expand_weight, reduce_weight, vectors, bias_table, attention_mean, attention_square, expand_mean, expand_square, reduce_mean, reduce_square, vectors_mean, vectors_square, table_mean, table_square):
    matrices = (attention_weight.astype(jnp.bfloat16), expand_weight.astype(jnp.bfloat16), reduce_weight.astype(jnp.bfloat16))
    row_vectors_list = lax.optimization_barrier(vectors.astype(jnp.bfloat16)).astype(jnp.float32)
    pos_bias = jnp.transpose(bias_table[relative_index], (2, 0, 1))
    region_windows = to_windows(region_ids[None])
    same_region = region_windows[:, :, None] == region_windows[:, None, :]
    window_size = WIN * WIN

    def shift_in(image):
        return to_windows(jnp.roll(image, (-SHIFT, -SHIFT), axis=(0, 1))[None])

    def shift_out(rows_flat):
        frame = from_windows(rows_flat.reshape(-1, window_size, C), 1, H, W)[0]
        return jnp.roll(frame, (SHIFT, SHIFT), axis=(0, 1))

    def per_image(running, inputs_pair):
        image, grad_image = inputs_pair
        output, stored_tensors = forward(shift_in(image), same_region, matrices, row_vectors_list, pos_bias)
        gradient_token_rows, gradients = backward(stored_tensors, shift_in(grad_image), same_region, matrices, row_vectors_list, pos_bias)
        running = tuple((total + term for total, term in zip(running, gradients)))
        return (running, (shift_out(output), shift_out(gradient_token_rows)))
    start = (jnp.zeros((C, 4 * C), jnp.float32), jnp.zeros((C, FFN), jnp.float32), jnp.zeros((FFN, C), jnp.float32), jnp.zeros((12, C), jnp.float32), jnp.zeros((HEADS, window_size, window_size), jnp.float32))
    sums, (block_output, input_grad) = lax.scan(per_image, start, (block_input, output_grad))
    inv_root = 1.0 / math.sqrt(IMAGES * H * W)
    attention_grad = sums[0] * inv_root
    expand_grad = sums[1] * inv_root
    reduce_grad = sums[2] * inv_root
    vectors_grad = sums[3] * inv_root
    table_grad = jax.ops.segment_sum(sums[4].reshape(HEADS, window_size * window_size).T, relative_index.reshape(-1).astype(jnp.int32), num_segments=TABLE) * inv_root
    new_attention, new_attention_mean, new_attention_square = adamw(attention_weight, attention_grad, attention_mean, attention_square, WEIGHT_DECAY)
    new_expand, new_expand_mean, new_expand_square = adamw(expand_weight, expand_grad, expand_mean, expand_square, WEIGHT_DECAY)
    new_reduce, new_reduce_mean, new_reduce_square = adamw(reduce_weight, reduce_grad, reduce_mean, reduce_square, WEIGHT_DECAY)
    new_vectors, new_vectors_mean, new_vectors_square = adamw(vectors, vectors_grad, vectors_mean, vectors_square, 0.0)
    new_table, new_table_mean, new_table_square = adamw(bias_table, table_grad, table_mean, table_square, 0.0)
    return (block_output, input_grad, attention_grad, expand_grad, reduce_grad, vectors_grad, table_grad, new_attention, new_expand, new_reduce, new_vectors, new_table, new_attention_mean, new_attention_square, new_expand_mean, new_expand_square, new_reduce_mean, new_reduce_square, new_vectors_mean, new_vectors_square, new_table_mean, new_table_square)
```

```python
import math

import jax
import jax.numpy as jnp
from jax import lax
from jax.experimental import pallas as pl
from jax.experimental.pallas import tpu as pltpu
from jax.sharding import PartitionSpec as P

WIN = 7
SHIFT = 3
STEP = 5


NORM_EPS = 1e-05
LEARN_RATE = 0.02
BETA_ONE = 0.9
BETA_TWO = 0.999
ADAM_EPS = 1e-08
WEIGHT_DECAY = 0.05
MASK_VALUE = -1000000000.0


BF = jnp.bfloat16
F32 = jnp.float32
MESH_ID = pl.DeviceIdType.MESH


def ring_position(index, count):
    column, row = index % 2, index // 2
    return (1 - column) * row + column * (count - 1 - row)


def ring_index(position, count):
    back = position // (count // 2)
    return (1 - back) * (2 * position) + back * (2 * (count - 1 - position) + 1)


def remote(src, dst, send, recv, **where):
    return pltpu.make_async_remote_copy(
        src_ref=src, dst_ref=dst, send_sem=send, recv_sem=recv, device_id=where, device_id_type=MESH_ID
    )


def greet(places):
    barrier = pltpu.get_barrier_semaphore()
    for where in places:
        pl.semaphore_signal(barrier, inc=1, device_id=where, device_id_type=MESH_ID)
    pl.semaphore_wait(barrier, len(places))


def gather_kernel(
    count, att, exp, red, vec, out_att, out_exp, out_red, out_vec,
    ring_send, ring_recv, pair_send, pair_recv, vec_send, vec_recv, own_sem,
):
    shard = lax.axis_index("shard")
    band = lax.axis_index("band")
    core = band % 2
    partner = band + 1 - 2 * core
    pos = ring_position(shard, count)
    to_right = ring_index((pos + 1) % count, count)
    to_left = ring_index((pos + count - 1) % count, count)
    peers = [(shard + j) % count for j in range(1, count)]
    greet([{"shard": peer} for peer in peers] + [{"band": partner}])

    def parts(block, quarter):
        lanes = pl.ds(pl.multiple_of(quarter * 512, 512), 512)
        return (
            out_att.at[block, :, lanes],
            out_exp.at[block, :, lanes],
            out_red.at[block, quarter],
        )

    def own_parts(quarter):
        lanes = pl.ds(pl.multiple_of(quarter * 512, 512), 512)
        return (att.at[:, lanes], exp.at[:, lanes], red.at[quarter])

    sends = []

    def send_ring(way, step):
        quarter = 2 * core + way
        block = ring_index((pos - step + count) % count if way == 0 else (pos + step) % count, count)
        target = to_right if way == 0 else to_left
        sources = own_parts(quarter) if step == 0 else parts(block, quarter)
        for k, (source, place) in enumerate(zip(sources, parts(block, quarter))):
            copy = remote(source, place, ring_send.at[way, step, k], ring_recv.at[way, step, k], shard=target)
            copy.start()
            sends.append(copy)

    for way in range(2):
        send_ring(way, 0)
    own = [
        pltpu.make_async_copy(source, place, own_sem.at[k])
        for k, (source, place) in enumerate(
            ((att, out_att.at[shard]), (exp, out_exp.at[shard]), (red, out_red.at[shard]), (vec, out_vec.at[shard]))
        )
    ]
    for copy in own:
        copy.start()
    for peer, j in zip(peers, range(count - 1)):
        copy = remote(vec, out_vec.at[shard], vec_send.at[j], vec_recv.at[j], shard=peer)
        copy.start()
        sends.append(copy)
    for step in range(count - 1):
        for way in range(2):
            quarter = 2 * core + way
            block = ring_index(
                (pos - step - 1 + count) % count if way == 0 else (pos + step + 1) % count, count
            )
            places = parts(block, quarter)
            for k, place in enumerate(places):
                remote(
                    place, place, ring_send.at[way, step, k], ring_recv.at[way, step, k], shard=to_right
                ).wait_recv()
            if step < count - 2:
                send_ring(way, step + 1)
            for k, place in enumerate(places):
                copy = remote(place, place, pair_send.at[way, step, k], pair_recv.at[way, step, k], band=partner)
                copy.start()
                sends.append(copy)
    for step in range(count - 1):
        for way in range(2):
            quarter = 2 * (1 - core) + way
            block = ring_index(
                (pos - step - 1 + count) % count if way == 0 else (pos + step + 1) % count, count
            )
            for k, place in enumerate(parts(block, quarter)):
                remote(
                    place, place, pair_send.at[way, step, k], pair_recv.at[way, step, k], band=partner
                ).wait_recv()
    for j in range(count - 1):
        source = (shard + count - 1 - j) % count
        remote(vec, out_vec.at[source], vec_send.at[j], vec_recv.at[j], shard=source).wait_recv()
    for copy in sends:
        copy.wait_send()
    for copy in own:
        copy.wait()


VM = pl.BlockSpec(memory_space=pltpu.VMEM)


def gather_shards(att, exp, red, vec):
    count = lax.axis_size("shard")
    rows = att.shape[0]
    dma = pltpu.SemaphoreType.DMA
    return pl.pallas_call(
        lambda *refs: gather_kernel(count, *refs),
        out_shape=(
            jax.ShapeDtypeStruct((count, rows, att.shape[1]), BF),
            jax.ShapeDtypeStruct((count, rows, exp.shape[1]), BF),
            jax.ShapeDtypeStruct((count,) + red.shape, BF),
            jax.ShapeDtypeStruct((count,) + vec.shape, BF),
        ),
        in_specs=[VM] * 4,
        out_specs=[VM] * 4,
        scratch_shapes=[
            dma((2, count - 1, 3)), dma((2, count - 1, 3)), dma((2, count - 1, 3)), dma((2, count - 1, 3)),
            dma((count - 1,)), dma((count - 1,)), dma((4,)),
        ],
        compiler_params=pltpu.CompilerParams(
            collective_id=0, has_side_effects=True, vmem_limit_bytes=48 * 1024 * 1024
        ),
        name="gather_shards",
    )(att, exp, red, vec)


def reduce_kernel(
    count, bands, att, exp, red, small, out_att, out_exp, out_red, out_small,
    paired, sent, got, done, others, mixed, small_band, small_shard,
    pair_send, pair_recv, ring_send, ring_recv, far_send, far_recv, mix_send, mix_recv,
    sb_send, sb_recv, ss_send, ss_recv,
):
    shard = lax.axis_index("shard")
    band = lax.axis_index("band")
    core = band % 2
    partner = band + 1 - 2 * core
    pos = ring_position(shard, count)
    to_right = ring_index((pos + 1) % count, count)
    to_left = ring_index((pos + count - 1) % count, count)
    shard_peers = [(shard + j) % count for j in range(1, count)]
    band_peers = [(band + j) % bands for j in range(1, bands)]
    rows = att.shape[1]
    greet([{"shard": peer} for peer in shard_peers] + [{"band": peer} for peer in band_peers])

    def block_of(way, step):
        if way == 0:
            return ring_index((pos - 1 - step + 2 * count) % count, count)
        return ring_index((pos + 1 + step) % count, count)

    def own_parts(block, quarter):
        lanes = pl.ds(pl.multiple_of(quarter * 512, 512), 512)
        return (att.at[block, :, lanes], exp.at[block, :, lanes], red.at[block, quarter])

    waits = []

    def pair_copy(way, step, k):
        block = block_of(way, step)
        source = own_parts(block, 2 * (1 - core) + way)[k]
        return remote(
            source, paired.at[way, step, k], pair_send.at[way, step, k], pair_recv.at[way, step, k], band=partner
        )

    for step in range(count):
        for way in range(2):
            for k in range(3):
                copy = pair_copy(way, step, k)
                copy.start()
                waits.append(copy)
        if step == 0:
            small_band[band] = small[...]
            for j, peer in enumerate(band_peers):
                copy = remote(small, small_band.at[band], sb_send.at[j], sb_recv.at[j], band=peer)
                copy.start()
                waits.append(copy)

    for step in range(count):
        for way in range(2):
            block = block_of(way, step)
            quarter = 2 * core + way
            if step > 0:
                remote(
                    sent.at[way, step - 1], got.at[way, step - 1],
                    ring_send.at[way, step - 1], ring_recv.at[way, step - 1], shard=to_right,
                ).wait_recv()
            lanes = pl.ds(pl.multiple_of(quarter * 512, 512), 512)
            for k in range(3):
                pair_copy(way, step, k).wait_recv()
                mine = (
                    att[block, :, lanes] if k == 0 else exp[block, :, lanes] if k == 1 else red[block, quarter]
                )
                total = mine.astype(F32) + paired[way, step, k].astype(F32)
                if step > 0:
                    total = total + got[way, step - 1, k].astype(F32)
                if step < count - 1:
                    sent[way, step, k] = total.astype(BF)
                else:
                    done[way, k] = total.astype(BF)
            if step < count - 1:
                copy = remote(
                    sent.at[way, step], got.at[way, step], ring_send.at[way, step], ring_recv.at[way, step],
                    shard=to_right if way == 0 else to_left,
                )
            else:
                for j in range(1, bands // 2):
                    copy = remote(
                        done.at[way], others.at[j - 1, way], far_send.at[j - 1, way], far_recv.at[j - 1, way],
                        band=(band + 2 * j) % bands,
                    )
                    copy.start()
                    waits.append(copy)
                continue
            copy.start()
            waits.append(copy)
        if step == 0:
            for j in range(bands - 1):
                source = (band + bands - 1 - j) % bands
                remote(small, small_band.at[source], sb_send.at[j], sb_recv.at[j], band=source).wait_recv()
            total = small_band[0]
            for j in range(1, bands):
                total = total + small_band[j]
            small_shard[shard] = total
            for j, peer in enumerate(shard_peers):
                copy = remote(
                    small_shard.at[shard], small_shard.at[shard], ss_send.at[j], ss_recv.at[j], shard=peer
                )
                copy.start()
                waits.append(copy)

    for way in range(2):
        for j in range(1, bands // 2):
            remote(
                done.at[way], others.at[j - 1, way], far_send.at[j - 1, way], far_recv.at[j - 1, way], band=partner
            ).wait_recv()
        total = done[way].astype(F32)
        for j in range(1, bands // 2):
            total = total + others[j - 1, way].astype(F32)
        mixed[core, way] = total.astype(BF)
        copy = remote(
            mixed.at[core, way], mixed.at[core, way], mix_send.at[way], mix_recv.at[way], band=partner
        )
        copy.start()
        waits.append(copy)
    for j in range(count - 1):
        source = (shard + count - 1 - j) % count
        remote(small, small_shard.at[source], ss_send.at[j], ss_recv.at[j], shard=source).wait_recv()
    total = small_shard[0]
    for j in range(1, count):
        total = total + small_shard[j]
    out_small[...] = total
    for way in range(2):
        remote(
            mixed.at[core, way], mixed.at[1 - core, way], mix_send.at[way], mix_recv.at[way], band=partner
        ).wait_recv()
    for quarter in range(4):
        out_att[:, quarter * 512 : quarter * 512 + 512] = mixed[quarter // 2, quarter % 2, 0].astype(F32)
        out_exp[:, quarter * 512 : quarter * 512 + 512] = mixed[quarter // 2, quarter % 2, 1].astype(F32)
        out_red[quarter] = mixed[quarter // 2, quarter % 2, 2].astype(F32)
    for copy in waits:
        copy.wait_send()


def reduce_to_owners(att, exp, red, small):
    count = lax.axis_size("shard")
    bands = lax.axis_size("band")
    rows = att.shape[1]
    dma = pltpu.SemaphoreType.DMA
    far = max(bands // 2 - 1, 1)
    return pl.pallas_call(
        lambda *refs: reduce_kernel(count, bands, *refs),
        out_shape=(
            jax.ShapeDtypeStruct(att.shape[1:], F32),
            jax.ShapeDtypeStruct(exp.shape[1:], F32),
            jax.ShapeDtypeStruct(red.shape[1:], F32),
            jax.ShapeDtypeStruct(small.shape, F32),
        ),
        in_specs=[VM] * 4,
        out_specs=[VM] * 4,
        scratch_shapes=[
            pltpu.VMEM((2, count, 3, rows, 512), BF),
            pltpu.VMEM((2, count - 1, 3, rows, 512), BF),
            pltpu.VMEM((2, count - 1, 3, rows, 512), BF),
            pltpu.VMEM((2, 3, rows, 512), BF),
            pltpu.VMEM((far, 2, 3, rows, 512), BF),
            pltpu.VMEM((2, 2, 3, rows, 512), BF),
            pltpu.VMEM((bands,) + small.shape, F32),
            pltpu.VMEM((count,) + small.shape, F32),
            dma((2, count, 3)), dma((2, count, 3)), dma((2, count - 1)), dma((2, count - 1)),
            dma((far, 2)), dma((far, 2)), dma((2,)), dma((2,)),
            dma((bands - 1,)), dma((bands - 1,)), dma((count - 1,)), dma((count - 1,)),
        ],
        compiler_params=pltpu.CompilerParams(
            collective_id=1, has_side_effects=True, vmem_limit_bytes=48 * 1024 * 1024
        ),
        name="reduce_to_owners",
    )(att, exp, red, small)


def passed_along(block, axis, distance):
    devices = range(lax.axis_size(axis))
    route = [((i - distance) % len(devices), i) for i in devices]
    return lax.ppermute(block, axis, route)


def to_windows(frame):
    image_count, rows_total, cols_total = (frame.shape[0], frame.shape[1], frame.shape[2])
    trailing = frame.shape[3:]
    blocks = frame.reshape((image_count, rows_total // WIN, WIN, cols_total // WIN, WIN) + trailing)
    blocks = jnp.moveaxis(blocks, 3, 2)
    return blocks.reshape(
        (image_count * (rows_total // WIN) * (cols_total // WIN), WIN * WIN) + trailing
    )


def from_windows(blocks, image_count, rows_total, cols_total):
    trailing = blocks.shape[2:]
    frame = blocks.reshape((image_count, rows_total // WIN, cols_total // WIN, WIN, WIN) + trailing)
    frame = jnp.moveaxis(frame, 3, 2)
    return frame.reshape((image_count, rows_total, cols_total) + trailing)


def layer_normalize(values):
    center = jnp.mean(values, axis=-1, keepdims=True)
    centered = values - center
    variance = jnp.mean(centered * centered, axis=-1, keepdims=True)
    inverse_deviation = lax.rsqrt(variance + NORM_EPS)
    return (centered * inverse_deviation, inverse_deviation)


def normalize_backward(gradient_standardized, standardized_input, inverse_deviation):
    return inverse_deviation * (
        gradient_standardized
        - jnp.mean(gradient_standardized, axis=-1, keepdims=True)
        - standardized_input
        * jnp.mean(gradient_standardized * standardized_input, axis=-1, keepdims=True)
    )


def gelu_parts(hidden_pre):
    normal_cdf = 0.5 * (1.0 + lax.erf(hidden_pre * (1.0 / math.sqrt(2.0))))
    density = jnp.exp(-0.5 * hidden_pre * hidden_pre) * (1.0 / math.sqrt(2.0 * math.pi))
    return (hidden_pre * normal_cdf, normal_cdf + hidden_pre * density)


def window_scores(per_head_queries, per_head_keys, same_region, pos_bias):
    raw = jnp.einsum(
        "wihd,wjhd->whij", per_head_queries, per_head_keys, preferred_element_type=jnp.float32
    )
    return jnp.where(same_region[:, None], raw + pos_bias[None], MASK_VALUE)


def forward(windows_in, same_region, matrices, row_vectors_list, pos_bias):
    attention, expand, shrink = matrices
    window_count, window_size, features = windows_in.shape
    head_count = pos_bias.shape[0]
    head_width = features // head_count
    score_scale = 1.0 / math.sqrt(head_width)
    incoming_tokens = windows_in.reshape(window_count * window_size, features).astype(jnp.float32)
    first_standardized, first_inverse_deviation = layer_normalize(incoming_tokens)
    first_normalized = (
        first_standardized * (1.0 + row_vectors_list[0]) + row_vectors_list[1]
    ).astype(jnp.bfloat16)
    projected = jnp.dot(
        first_normalized, attention[:, : 3 * features], preferred_element_type=jnp.float32
    )
    head_shape = (window_count, window_size, head_count, head_width)
    per_head_queries = (
        ((projected[:, :features] + row_vectors_list[2]) * score_scale)
        .astype(jnp.bfloat16)
        .reshape(head_shape)
    )
    per_head_keys = projected[:, features : 2 * features].astype(jnp.bfloat16).reshape(head_shape)
    per_head_values = (
        (projected[:, 2 * features :] + row_vectors_list[3])
        .astype(jnp.bfloat16)
        .reshape(head_shape)
    )
    scores = window_scores(per_head_queries, per_head_keys, same_region, pos_bias)
    row_peak = jnp.max(scores, axis=-1, keepdims=True)
    powers = jnp.exp(scores - row_peak)
    totals = jnp.sum(powers, axis=-1, keepdims=True)
    logarithm_total = row_peak + jnp.log(totals)
    prob_b = (powers / totals).astype(jnp.bfloat16)
    attended = jnp.einsum(
        "whij,wjhd->wihd", prob_b, per_head_values, preferred_element_type=jnp.float32
    )
    attended_bfloat = attended.reshape(window_count * window_size, features).astype(jnp.bfloat16)
    residual_stream = (
        incoming_tokens
        + jnp.dot(attended_bfloat, attention[:, 3 * features :], preferred_element_type=jnp.float32)
        + row_vectors_list[4]
    )
    second_standardized, second_inverse_deviation = layer_normalize(residual_stream)
    second_normalized = (
        second_standardized * (1.0 + row_vectors_list[5]) + row_vectors_list[6]
    ).astype(jnp.bfloat16)
    hidden_pre = jnp.dot(
        second_normalized, expand, preferred_element_type=jnp.float32
    ) + row_vectors_list[8:].reshape(-1)
    activated, gaussian_unit_slope = gelu_parts(hidden_pre)
    activated_bfloat = activated.astype(jnp.bfloat16)
    output = (
        residual_stream
        + jnp.dot(activated_bfloat, shrink, preferred_element_type=jnp.float32)
        + row_vectors_list[7]
    )
    stored_tensors = (
        first_standardized,
        first_inverse_deviation,
        first_normalized,
        per_head_queries,
        per_head_keys,
        per_head_values,
        logarithm_total,
        attended_bfloat,
        second_standardized,
        second_inverse_deviation,
        second_normalized,
        gaussian_unit_slope,
        activated_bfloat,
    )
    return (output, stored_tensors)


def backward(stored_tensors, grad_windows, same_region, matrices, row_vectors_list, pos_bias):
    (
        first_standardized,
        first_inverse_deviation,
        first_normalized,
        per_head_queries,
        per_head_keys,
        per_head_values,
        logarithm_total,
        attended_bfloat,
        second_standardized,
        second_inverse_deviation,
        second_normalized,
        gaussian_unit_slope,
        activated_bfloat,
    ) = stored_tensors
    attention, expand, shrink = matrices
    window_count, window_size, head_count, head_width = per_head_queries.shape
    features = head_count * head_width
    score_scale = 1.0 / math.sqrt(head_width)
    rows_shape = (window_count * window_size, features)
    grad_rows = grad_windows.reshape(rows_shape)
    gradient_single_float = grad_rows.astype(jnp.float32)
    grad_obias = jnp.sum(gradient_single_float, axis=0)
    grad_shrink = jnp.dot(activated_bfloat.T, grad_rows, preferred_element_type=jnp.float32)
    grad_act = jnp.dot(grad_rows, shrink.T, preferred_element_type=jnp.float32)
    grad_pre = grad_act * gaussian_unit_slope
    grad_pre_b = grad_pre.astype(jnp.bfloat16)
    grad_ebias = jnp.sum(grad_pre, axis=0)
    grad_expand = jnp.dot(second_normalized.T, grad_pre_b, preferred_element_type=jnp.float32)
    gradient_second_normalized = jnp.dot(grad_pre_b, expand.T, preferred_element_type=jnp.float32)
    gradient_second_gain = jnp.sum(gradient_second_normalized * second_standardized, axis=0)
    grad_beta_two = jnp.sum(gradient_second_normalized, axis=0)
    gradient_residual_stream = gradient_single_float + normalize_backward(
        gradient_second_normalized * (1.0 + row_vectors_list[5]),
        second_standardized,
        second_inverse_deviation,
    )
    grad_resid_b = gradient_residual_stream.astype(jnp.bfloat16)
    grad_pbias = jnp.sum(gradient_residual_stream, axis=0)
    grad_outproj = jnp.dot(attended_bfloat.T, grad_resid_b, preferred_element_type=jnp.float32)
    head_shape = (window_count, window_size, head_count, head_width)
    grad_attended = (
        jnp.dot(grad_resid_b, attention[:, 3 * features :].T, preferred_element_type=jnp.float32)
        .astype(jnp.bfloat16)
        .reshape(head_shape)
    )
    scores = window_scores(per_head_queries, per_head_keys, same_region, pos_bias)
    prob_full = jnp.exp(scores - logarithm_total)
    prob_b = prob_full.astype(jnp.bfloat16)
    grad_probs = jnp.einsum(
        "wihd,wjhd->whij", grad_attended, per_head_values, preferred_element_type=jnp.float32
    )
    grad_value = jnp.einsum(
        "whij,wihd->wjhd", prob_b, grad_attended, preferred_element_type=jnp.float32
    )
    inner_sum = jnp.sum(prob_full * grad_probs, axis=-1, keepdims=True)
    grad_scores = prob_full * (grad_probs - inner_sum)
    grad_posbias = jnp.sum(grad_scores, axis=0)
    grad_scores_b = grad_scores.astype(jnp.bfloat16)
    grad_query = (
        jnp.einsum(
            "whij,wjhd->wihd", grad_scores_b, per_head_keys, preferred_element_type=jnp.float32
        )
        * score_scale
    )
    grad_key = jnp.einsum(
        "whij,wihd->wjhd", grad_scores_b, per_head_queries, preferred_element_type=jnp.float32
    )
    grad_query = grad_query.reshape(rows_shape)
    grad_value = grad_value.reshape(rows_shape)
    grad_qkv = jnp.concatenate([grad_query, grad_key.reshape(rows_shape), grad_value], axis=1)
    grad_qkv_b = grad_qkv.astype(jnp.bfloat16)
    grad_inproj = jnp.dot(first_normalized.T, grad_qkv_b, preferred_element_type=jnp.float32)
    gradient_first_normalized = jnp.dot(
        grad_qkv_b, attention[:, : 3 * features].T, preferred_element_type=jnp.float32
    )
    gradient_first_gain = jnp.sum(gradient_first_normalized * first_standardized, axis=0)
    grad_beta_one = jnp.sum(gradient_first_normalized, axis=0)
    gradient_token_rows = gradient_residual_stream + normalize_backward(
        gradient_first_normalized * (1.0 + row_vectors_list[0]),
        first_standardized,
        first_inverse_deviation,
    )
    grad_attention = jnp.concatenate([grad_inproj, grad_outproj], axis=1)
    grad_vectors = jnp.concatenate(
        [
            jnp.stack(
                [
                    gradient_first_gain,
                    grad_beta_one,
                    jnp.sum(grad_query, axis=0),
                    jnp.sum(grad_value, axis=0),
                    grad_pbias,
                    gradient_second_gain,
                    grad_beta_two,
                    grad_obias,
                ]
            ),
            grad_ebias.reshape(4, features),
        ],
        axis=0,
    )
    return (
        gradient_token_rows,
        (grad_attention, grad_expand, grad_shrink, grad_vectors, grad_posbias),
    )


def adamw(weight, grad, first, second, decay):
    first_new = BETA_ONE * first + (1.0 - BETA_ONE) * grad
    second_new = BETA_TWO * second + (1.0 - BETA_TWO) * grad * grad
    corr_one = 1.0 - BETA_ONE**STEP
    corr_two = 1.0 - BETA_TWO**STEP
    step_dir = first_new / corr_one / (jnp.sqrt(second_new / corr_two) + ADAM_EPS)
    return (weight - LEARN_RATE * (step_dir + decay * weight), first_new, second_new)


def on_device(
    block_input,
    output_grad,
    region_ids,
    relative_index,
    attention_weight,
    expand_weight,
    reduce_weight,
    vectors,
    bias_table,
    attention_mean,
    attention_square,
    expand_mean,
    expand_square,
    reduce_mean,
    reduce_square,
    vectors_mean,
    vectors_square,
    table_mean,
    table_square,
):
    image_count, band_rows, columns, features = block_input.shape
    window_size = WIN * WIN
    shard_count = lax.axis_size("shard")
    band_count = lax.axis_size("band")
    edge_rows = jnp.stack([block_input[:, :SHIFT], output_grad[:, :SHIFT]])
    rows_below = passed_along(edge_rows, "band", -1)
    inner_rows = jnp.stack([block_input[:, SHIFT:], output_grad[:, SHIFT:]])
    shifted = jnp.roll(jnp.concatenate([inner_rows, rows_below], axis=2), -SHIFT, axis=3)
    windows_in = to_windows(shifted[0])
    grad_windows = to_windows(shifted[1])
    region_windows = jnp.tile(to_windows(region_ids[None]), (image_count, 1))
    same_region = region_windows[:, :, None] == region_windows[:, None, :]
    table_rows = bias_table.shape[0]
    head_count = bias_table.shape[1]
    one_hot = (
        relative_index.reshape(-1)[:, None] == jnp.arange(table_rows, dtype=jnp.int32)[None, :]
    ).astype(jnp.float32)
    pos_bias = jnp.dot(one_hot, bias_table, precision=lax.Precision.HIGHEST).T.reshape(
        head_count, window_size, window_size
    )
    feature_rows = attention_weight.shape[0]
    gathered = gather_shards(
        attention_weight.astype(BF),
        expand_weight.astype(BF),
        reduce_weight.astype(BF).reshape(4, feature_rows, features),
        jnp.pad(vectors.astype(BF), ((0, 4), (0, 128 - vectors.shape[1]))),
    )
    matrices = (
        gathered[0].reshape(features, -1),
        gathered[1].reshape(features, -1),
        gathered[2].reshape(-1, features),
    )
    row_vectors_list = (
        jnp.moveaxis(gathered[3][:, :12, : vectors.shape[1]], 0, 1).reshape(12, features).astype(jnp.float32)
    )
    output_rows, stored_tensors = forward(
        windows_in, same_region, matrices, row_vectors_list, pos_bias
    )
    gradient_token_rows, gradients = backward(
        stored_tensors, grad_windows, same_region, matrices, row_vectors_list, pos_bias
    )
    grad_attention, grad_expand, grad_shrink, grad_vectors, grad_posbias = gradients
    inv_root = 1.0 / math.sqrt(image_count * shard_count * band_rows * band_count * columns)
    table_local = jnp.dot(
        grad_posbias.reshape(head_count, -1), one_hot, precision=lax.Precision.HIGHEST
    ).T
    vector_terms = grad_vectors.size
    small = jnp.concatenate([grad_vectors.reshape(-1), table_local.reshape(-1)]) * inv_root
    small_rows = -(-small.size // 1024) * 8
    small = jnp.pad(small, (0, small_rows * 128 - small.size)).reshape(small_rows, 128)
    attention_grad, expand_grad, reduce_grad, small_sum = reduce_to_owners(
        (grad_attention * inv_root).astype(BF).reshape(shard_count, feature_rows, -1),
        (grad_expand * inv_root).astype(BF).reshape(shard_count, feature_rows, -1),
        (grad_shrink * inv_root).astype(BF).reshape(shard_count, 4, feature_rows, features),
        small,
    )
    reduce_grad = reduce_grad.reshape(reduce_weight.shape)
    small_sum = small_sum.reshape(-1)
    vectors_grad = lax.dynamic_slice_in_dim(
        small_sum[:vector_terms].reshape(12, features),
        lax.axis_index("shard") * vectors.shape[1],
        vectors.shape[1],
        axis=1,
    )
    table_grad = small_sum[vector_terms : vector_terms + bias_table.size].reshape(bias_table.shape)
    frames = jnp.stack(
        [
            from_windows(
                output_rows.reshape(-1, window_size, features), image_count, band_rows, columns
            ),
            from_windows(
                gradient_token_rows.reshape(-1, window_size, features),
                image_count,
                band_rows,
                columns,
            ),
        ]
    )
    frames = jnp.roll(frames, SHIFT, axis=3)
    rows_above = passed_along(
        frames[:, :, band_rows - SHIFT :].astype(jnp.bfloat16), "band", 1
    ).astype(jnp.float32)
    placed = jnp.concatenate([rows_above, frames[:, :, : band_rows - SHIFT]], axis=2)
    new_attention, new_attention_mean, new_attention_square = adamw(
        attention_weight, attention_grad, attention_mean, attention_square, WEIGHT_DECAY
    )
    new_expand, new_expand_mean, new_expand_square = adamw(
        expand_weight, expand_grad, expand_mean, expand_square, WEIGHT_DECAY
    )
    new_reduce, new_reduce_mean, new_reduce_square = adamw(
        reduce_weight, reduce_grad, reduce_mean, reduce_square, WEIGHT_DECAY
    )
    new_vectors, new_vectors_mean, new_vectors_square = adamw(
        vectors, vectors_grad, vectors_mean, vectors_square, 0.0
    )
    new_table, new_table_mean, new_table_square = adamw(
        bias_table, table_grad, table_mean, table_square, 0.0
    )
    return (
        placed[0],
        placed[1],
        attention_grad,
        expand_grad,
        reduce_grad,
        vectors_grad,
        table_grad,
        new_attention,
        new_expand,
        new_reduce,
        new_vectors,
        new_table,
        new_attention_mean,
        new_attention_square,
        new_expand_mean,
        new_expand_square,
        new_reduce_mean,
        new_reduce_square,
        new_vectors_mean,
        new_vectors_square,
        new_table_mean,
        new_table_square,
    )


def solution(mesh):
    return jax.shard_map(
        on_device,
        mesh=mesh,
        in_specs=(
            P("shard", "band", None, None),
            P("shard", "band", None, None),
            P("band", None),
            P(),
            P("shard", None),
            P("shard", None),
            P("shard", None),
            P(None, "shard"),
            P(),
            P("shard", None),
            P("shard", None),
            P("shard", None),
            P("shard", None),
            P("shard", None),
            P("shard", None),
            P(None, "shard"),
            P(None, "shard"),
            P(),
            P(),
        ),
        out_specs=(
            P("shard", "band", None, None),
            P("shard", "band", None, None),
            P("shard", None),
            P("shard", None),
            P("shard", None),
            P(None, "shard"),
            P(),
            P("shard", None),
            P("shard", None),
            P("shard", None),
            P(None, "shard"),
            P(),
            P("shard", None),
            P("shard", None),
            P("shard", None),
            P("shard", None),
            P("shard", None),
            P("shard", None),
            P(None, "shard"),
            P(None, "shard"),
            P(),
            P(),
        ),
        check_vma=False,
    )
```

```python
import math

import jax
import jax.numpy as jnp
from jax import lax
from jax.experimental import pallas as pl
from jax.experimental.pallas import tpu as pltpu
from jax.sharding import PartitionSpec as P

WIN = 7
SHIFT = 3
STEP = 5


NORM_EPS = 1e-05
LEARN_RATE = 0.02
BETA_ONE = 0.9
BETA_TWO = 0.999
ADAM_EPS = 1e-08
WEIGHT_DECAY = 0.05
MASK_VALUE = -1000000000.0


BF = jnp.bfloat16
F32 = jnp.float32
MESH_ID = pl.DeviceIdType.MESH


def ring_position(index, count):
    column, row = index % 2, index // 2
    return (1 - column) * row + column * (count - 1 - row)


def ring_index(position, count):
    back = position // (count // 2)
    return (1 - back) * (2 * position) + back * (2 * (count - 1 - position) + 1)


def remote(src, dst, send, recv, **where):
    return pltpu.make_async_remote_copy(
        src_ref=src, dst_ref=dst, send_sem=send, recv_sem=recv, device_id=where, device_id_type=MESH_ID
    )


def greet(places):
    barrier = pltpu.get_barrier_semaphore()
    for where in places:
        pl.semaphore_signal(barrier, inc=1, device_id=where, device_id_type=MESH_ID)
    pl.semaphore_wait(barrier, len(places))


def gather_kernel(
    count, att, exp, red, vec, out_att, out_exp, out_red, out_vec,
    ring_send, ring_recv, pair_send, pair_recv, vec_send, vec_recv, own_sem,
):
    shard = lax.axis_index("shard")
    band = lax.axis_index("band")
    core = band % 2
    partner = band + 1 - 2 * core
    pos = ring_position(shard, count)
    to_right = ring_index((pos + 1) % count, count)
    to_left = ring_index((pos + count - 1) % count, count)
    peers = [(shard + j) % count for j in range(1, count)]
    greet([{"shard": peer} for peer in peers] + [{"band": partner}])

    def parts(block, quarter):
        lanes = pl.ds(pl.multiple_of(quarter * 512, 512), 512)
        return (
            out_att.at[block, :, lanes],
            out_exp.at[block, :, lanes],
            out_red.at[block, quarter],
        )

    def own_parts(quarter):
        lanes = pl.ds(pl.multiple_of(quarter * 512, 512), 512)
        return (att.at[:, lanes], exp.at[:, lanes], red.at[quarter])

    sends = []

    def send_ring(way, step):
        quarter = 2 * core + way
        block = ring_index((pos - step + count) % count if way == 0 else (pos + step) % count, count)
        target = to_right if way == 0 else to_left
        sources = own_parts(quarter) if step == 0 else parts(block, quarter)
        for k, (source, place) in enumerate(zip(sources, parts(block, quarter))):
            copy = remote(source, place, ring_send.at[way, step, k], ring_recv.at[way, step, k], shard=target)
            copy.start()
            sends.append(copy)

    for way in range(2):
        send_ring(way, 0)
    own = [
        pltpu.make_async_copy(source, place, own_sem.at[k])
        for k, (source, place) in enumerate(
            ((att, out_att.at[shard]), (exp, out_exp.at[shard]), (red, out_red.at[shard]), (vec, out_vec.at[shard]))
        )
    ]
    for copy in own:
        copy.start()
    for peer, j in zip(peers, range(count - 1)):
        copy = remote(vec, out_vec.at[shard], vec_send.at[j], vec_recv.at[j], shard=peer)
        copy.start()
        sends.append(copy)
    for step in range(count - 1):
        for way in range(2):
            quarter = 2 * core + way
            block = ring_index(
                (pos - step - 1 + count) % count if way == 0 else (pos + step + 1) % count, count
            )
            places = parts(block, quarter)
            for k, place in enumerate(places):
                remote(
                    place, place, ring_send.at[way, step, k], ring_recv.at[way, step, k], shard=to_right
                ).wait_recv()
            if step < count - 2:
                send_ring(way, step + 1)
            for k, place in enumerate(places):
                copy = remote(place, place, pair_send.at[way, step, k], pair_recv.at[way, step, k], band=partner)
                copy.start()
                sends.append(copy)
    for step in range(count - 1):
        for way in range(2):
            quarter = 2 * (1 - core) + way
            block = ring_index(
                (pos - step - 1 + count) % count if way == 0 else (pos + step + 1) % count, count
            )
            for k, place in enumerate(parts(block, quarter)):
                remote(
                    place, place, pair_send.at[way, step, k], pair_recv.at[way, step, k], band=partner
                ).wait_recv()
    for j in range(count - 1):
        source = (shard + count - 1 - j) % count
        remote(vec, out_vec.at[source], vec_send.at[j], vec_recv.at[j], shard=source).wait_recv()
    for copy in sends:
        copy.wait_send()
    for copy in own:
        copy.wait()


VM = pl.BlockSpec(memory_space=pltpu.VMEM)


def gather_shards(att, exp, red, vec):
    count = lax.axis_size("shard")
    rows = att.shape[0]
    dma = pltpu.SemaphoreType.DMA
    return pl.pallas_call(
        lambda *refs: gather_kernel(count, *refs),
        out_shape=(
            jax.ShapeDtypeStruct((count, rows, att.shape[1]), BF),
            jax.ShapeDtypeStruct((count, rows, exp.shape[1]), BF),
            jax.ShapeDtypeStruct((count,) + red.shape, BF),
            jax.ShapeDtypeStruct((count,) + vec.shape, BF),
        ),
        in_specs=[VM] * 4,
        out_specs=[VM] * 4,
        scratch_shapes=[
            dma((2, count - 1, 3)), dma((2, count - 1, 3)), dma((2, count - 1, 3)), dma((2, count - 1, 3)),
            dma((count - 1,)), dma((count - 1,)), dma((4,)),
        ],
        compiler_params=pltpu.CompilerParams(
            collective_id=0, has_side_effects=True, vmem_limit_bytes=48 * 1024 * 1024
        ),
        name="gather_shards",
    )(att, exp, red, vec)


def reduce_kernel(
    count, bands, att, exp, red, small, out_att, out_exp, out_red, out_small,
    paired, sent, got, done, others, mixed, small_band, small_shard,
    pair_send, pair_recv, ring_send, ring_recv, far_send, far_recv, mix_send, mix_recv,
    sb_send, sb_recv, ss_send, ss_recv,
):
    shard = lax.axis_index("shard")
    band = lax.axis_index("band")
    core = band % 2
    partner = band + 1 - 2 * core
    pos = ring_position(shard, count)
    to_right = ring_index((pos + 1) % count, count)
    to_left = ring_index((pos + count - 1) % count, count)
    shard_peers = [(shard + j) % count for j in range(1, count)]
    band_peers = [(band + j) % bands for j in range(1, bands)]
    rows = att.shape[1]
    greet([{"shard": peer} for peer in shard_peers] + [{"band": peer} for peer in band_peers])

    def block_of(way, step):
        if way == 0:
            return ring_index((pos - 1 - step + 2 * count) % count, count)
        return ring_index((pos + 1 + step) % count, count)

    def own_parts(block, quarter):
        lanes = pl.ds(pl.multiple_of(quarter * 512, 512), 512)
        return (att.at[block, :, lanes], exp.at[block, :, lanes], red.at[block, quarter])

    waits = []

    def pair_copy(way, step, k):
        block = block_of(way, step)
        source = own_parts(block, 2 * (1 - core) + way)[k]
        return remote(
            source, paired.at[way, step, k], pair_send.at[way, step, k], pair_recv.at[way, step, k], band=partner
        )

    for step in range(count):
        for way in range(2):
            for k in range(3):
                copy = pair_copy(way, step, k)
                copy.start()
                waits.append(copy)
        if step == 0:
            small_band[band] = small[...]
            for j, peer in enumerate(band_peers):
                copy = remote(small, small_band.at[band], sb_send.at[j], sb_recv.at[j], band=peer)
                copy.start()
                waits.append(copy)

    for step in range(count):
        for way in range(2):
            block = block_of(way, step)
            quarter = 2 * core + way
            if step > 0:
                remote(
                    sent.at[way, step - 1], got.at[way, step - 1],
                    ring_send.at[way, step - 1], ring_recv.at[way, step - 1], shard=to_right,
                ).wait_recv()
            lanes = pl.ds(pl.multiple_of(quarter * 512, 512), 512)
            for k in range(3):
                pair_copy(way, step, k).wait_recv()
                mine = (
                    att[block, :, lanes] if k == 0 else exp[block, :, lanes] if k == 1 else red[block, quarter]
                )
                total = mine.astype(F32) + paired[way, step, k].astype(F32)
                if step > 0:
                    total = total + got[way, step - 1, k].astype(F32)
                if step < count - 1:
                    sent[way, step, k] = total.astype(BF)
                else:
                    done[way, k] = total.astype(BF)
            if step < count - 1:
                copy = remote(
                    sent.at[way, step], got.at[way, step], ring_send.at[way, step], ring_recv.at[way, step],
                    shard=to_right if way == 0 else to_left,
                )
            else:
                for j in range(1, bands // 2):
                    copy = remote(
                        done.at[way], others.at[j - 1, way], far_send.at[j - 1, way], far_recv.at[j - 1, way],
                        band=(band + 2 * j) % bands,
                    )
                    copy.start()
                    waits.append(copy)
                continue
            copy.start()
            waits.append(copy)
        if step == 0:
            for j in range(bands - 1):
                source = (band + bands - 1 - j) % bands
                remote(small, small_band.at[source], sb_send.at[j], sb_recv.at[j], band=source).wait_recv()
            total = small_band[0]
            for j in range(1, bands):
                total = total + small_band[j]
            small_shard[shard] = total
            for j, peer in enumerate(shard_peers):
                copy = remote(
                    small_shard.at[shard], small_shard.at[shard], ss_send.at[j], ss_recv.at[j], shard=peer
                )
                copy.start()
                waits.append(copy)

    for way in range(2):
        for j in range(1, bands // 2):
            remote(
                done.at[way], others.at[j - 1, way], far_send.at[j - 1, way], far_recv.at[j - 1, way], band=partner
            ).wait_recv()
        total = done[way].astype(F32)
        for j in range(1, bands // 2):
            total = total + others[j - 1, way].astype(F32)
        mixed[core, way] = total.astype(BF)
        copy = remote(
            mixed.at[core, way], mixed.at[core, way], mix_send.at[way], mix_recv.at[way], band=partner
        )
        copy.start()
        waits.append(copy)
    for j in range(count - 1):
        source = (shard + count - 1 - j) % count
        remote(small, small_shard.at[source], ss_send.at[j], ss_recv.at[j], shard=source).wait_recv()
    total = small_shard[0]
    for j in range(1, count):
        total = total + small_shard[j]
    out_small[...] = total
    for way in range(2):
        remote(
            mixed.at[core, way], mixed.at[1 - core, way], mix_send.at[way], mix_recv.at[way], band=partner
        ).wait_recv()
    for quarter in range(4):
        out_att[:, quarter * 512 : quarter * 512 + 512] = mixed[quarter // 2, quarter % 2, 0].astype(F32)
        out_exp[:, quarter * 512 : quarter * 512 + 512] = mixed[quarter // 2, quarter % 2, 1].astype(F32)
        out_red[quarter] = mixed[quarter // 2, quarter % 2, 2].astype(F32)
    for copy in waits:
        copy.wait_send()


def reduce_to_owners(att, exp, red, small):
    count = lax.axis_size("shard")
    bands = lax.axis_size("band")
    rows = att.shape[1]
    dma = pltpu.SemaphoreType.DMA
    far = max(bands // 2 - 1, 1)
    return pl.pallas_call(
        lambda *refs: reduce_kernel(count, bands, *refs),
        out_shape=(
            jax.ShapeDtypeStruct(att.shape[1:], F32),
            jax.ShapeDtypeStruct(exp.shape[1:], F32),
            jax.ShapeDtypeStruct(red.shape[1:], F32),
            jax.ShapeDtypeStruct(small.shape, F32),
        ),
        in_specs=[VM] * 4,
        out_specs=[VM] * 4,
        scratch_shapes=[
            pltpu.VMEM((2, count, 3, rows, 512), BF),
            pltpu.VMEM((2, count - 1, 3, rows, 512), BF),
            pltpu.VMEM((2, count - 1, 3, rows, 512), BF),
            pltpu.VMEM((2, 3, rows, 512), BF),
            pltpu.VMEM((far, 2, 3, rows, 512), BF),
            pltpu.VMEM((2, 2, 3, rows, 512), BF),
            pltpu.VMEM((bands,) + small.shape, F32),
            pltpu.VMEM((count,) + small.shape, F32),
            dma((2, count, 3)), dma((2, count, 3)), dma((2, count - 1)), dma((2, count - 1)),
            dma((far, 2)), dma((far, 2)), dma((2,)), dma((2,)),
            dma((bands - 1,)), dma((bands - 1,)), dma((count - 1,)), dma((count - 1,)),
        ],
        compiler_params=pltpu.CompilerParams(
            collective_id=1, has_side_effects=True, vmem_limit_bytes=48 * 1024 * 1024
        ),
        name="reduce_to_owners",
    )(att, exp, red, small)


def passed_along(block, axis, distance):
    devices = range(lax.axis_size(axis))
    route = [((i - distance) % len(devices), i) for i in devices]
    return lax.ppermute(block, axis, route)


def to_windows(frame):
    image_count, rows_total, cols_total = (frame.shape[0], frame.shape[1], frame.shape[2])
    trailing = frame.shape[3:]
    blocks = frame.reshape((image_count, rows_total // WIN, WIN, cols_total // WIN, WIN) + trailing)
    blocks = jnp.moveaxis(blocks, 3, 2)
    return blocks.reshape(
        (image_count * (rows_total // WIN) * (cols_total // WIN), WIN * WIN) + trailing
    )


def from_windows(blocks, image_count, rows_total, cols_total):
    trailing = blocks.shape[2:]
    frame = blocks.reshape((image_count, rows_total // WIN, cols_total // WIN, WIN, WIN) + trailing)
    frame = jnp.moveaxis(frame, 3, 2)
    return frame.reshape((image_count, rows_total, cols_total) + trailing)


def layer_normalize(values):
    center = jnp.mean(values, axis=-1, keepdims=True)
    centered = values - center
    variance = jnp.mean(centered * centered, axis=-1, keepdims=True)
    inverse_deviation = lax.rsqrt(variance + NORM_EPS)
    return (centered * inverse_deviation, inverse_deviation)


def normalize_backward(gradient_standardized, standardized_input, inverse_deviation):
    return inverse_deviation * (
        gradient_standardized
        - jnp.mean(gradient_standardized, axis=-1, keepdims=True)
        - standardized_input
        * jnp.mean(gradient_standardized * standardized_input, axis=-1, keepdims=True)
    )


def gelu_parts(hidden_pre):
    normal_cdf = 0.5 * (1.0 + lax.erf(hidden_pre * (1.0 / math.sqrt(2.0))))
    density = jnp.exp(-0.5 * hidden_pre * hidden_pre) * (1.0 / math.sqrt(2.0 * math.pi))
    return (hidden_pre * normal_cdf, normal_cdf + hidden_pre * density)


def adamw(weight, grad, first, second, decay):
    first_new = BETA_ONE * first + (1.0 - BETA_ONE) * grad
    second_new = BETA_TWO * second + (1.0 - BETA_TWO) * grad * grad
    corr_one = 1.0 - BETA_ONE**STEP
    corr_two = 1.0 - BETA_TWO**STEP
    step_dir = first_new / corr_one / (jnp.sqrt(second_new / corr_two) + ADAM_EPS)
    return (weight - LEARN_RATE * (step_dir + decay * weight), first_new, second_new)


PADDED = 64
GROUP = 128


def dot_nn(a, b):
    return jnp.dot(a, b, preferred_element_type=F32)


def dot_tn(a, b):
    return lax.dot_general(a, b, (((0,), (0,)), ((), ())), preferred_element_type=F32)


def dot_nt(a, b):
    return lax.dot_general(a, b, (((1,), (1,)), ((), ())), preferred_element_type=F32)


def block_kernel(
    inv_root, x_ref, d_ref, att, exp, red, vec, bias, same,
    out_y, out_dt, g_att, g_exp, g_red, g_vec, g_bias,
    xhat1, q_s, k_s, v_s, h1_s, o_s, do_s, p_s, dqkv_s, r1_s, dr1_s,
):
    rows, width = x_ref.shape
    windows = rows // PADDED
    heads = bias.shape[0]
    head_width = width // heads
    stacked = GROUP // head_width
    groups = width // GROUP
    scale = 1.0 / math.sqrt(head_width)

    def row(k):
        return vec[k : k + 1, :]

    def normed(values):
        centered = values - jnp.mean(values, axis=-1, keepdims=True)
        inverse = lax.rsqrt(jnp.mean(centered * centered, axis=-1, keepdims=True) + NORM_EPS)
        return centered * inverse, inverse

    def put(ref, value, lanes=None):
        value = (value * inv_root).astype(BF)
        if lanes is None:
            ref[...] = value
        else:
            ref[:, lanes] = value

    def column_sum(k, value):
        g_vec[k : k + 1, :] = jnp.sum(value, axis=0, keepdims=True)

    lane = lax.broadcasted_iota(jnp.int32, (1, GROUP), 1) // head_width

    def stack_heads(block):
        zero = jnp.zeros_like(block)
        return jnp.concatenate([jnp.where(lane == h, block, zero) for h in range(stacked)], axis=0)

    def pick_heads(block):
        total = jnp.where(lane == 0, block[:PADDED], 0.0)
        for h in range(1, stacked):
            total = jnp.where(lane == h, block[h * PADDED : (h + 1) * PADDED], total)
        return total

    g_vec[...] = jnp.zeros_like(g_vec)
    standard, inverse1 = normed(x_ref[...].astype(F32))
    xhat1[...] = standard
    h1_s[...] = (standard * (1.0 + row(0)) + row(1)).astype(BF)
    q_s[...] = ((dot_nn(h1_s[...], att[:, :width]) + row(2)) * scale).astype(BF)
    k_s[...] = dot_nn(h1_s[...], att[:, width : 2 * width]).astype(BF)
    v_s[...] = (dot_nn(h1_s[...], att[:, 2 * width : 3 * width]) + row(3)).astype(BF)

    def attend(w, carry):
        here = pl.ds(pl.multiple_of(w * PADDED, PADDED), PADDED)
        allowed = same[w] > 0.5
        allowed = jnp.concatenate([same[w]] * stacked, axis=0) > 0.5
        for g in range(groups):
            lanes = slice(g * GROUP, (g + 1) * GROUP)
            scores = dot_nt(stack_heads(q_s[here, lanes]), k_s[here, lanes])
            shift = jnp.concatenate([bias[g * stacked + h] for h in range(stacked)], axis=0)
            scores = jnp.where(allowed, scores + shift, MASK_VALUE)
            powers = jnp.exp(scores - jnp.max(scores, axis=-1, keepdims=True))
            prob = powers / jnp.sum(powers, axis=-1, keepdims=True)
            p_s[w, g] = prob
            o_s[here, lanes] = pick_heads(dot_nn(prob.astype(BF), v_s[here, lanes])).astype(BF)
        return carry

    lax.fori_loop(0, windows, attend, 0)

    r1_s[...] = x_ref[...].astype(F32) + dot_nn(o_s[...], att[:, 3 * width :]) + row(4)
    xhat2, inverse2 = normed(r1_s[...])
    h2 = (xhat2 * (1.0 + row(5)) + row(6)).astype(BF)
    d_b = d_ref[...]
    d = d_b.astype(F32)
    column_sum(7, d)
    out_y[...] = r1_s[...] + row(7)
    chunks = exp.shape[1] // width
    for c in range(chunks):
        lanes = slice(c * width, (c + 1) * width)
        pre = dot_nn(h2, exp[:, lanes]) + row(8 + c)
        activated, slope = gelu_parts(pre)
        z = activated.astype(BF)
        out_y[...] += dot_nn(z, red[lanes, :])
        g_red[lanes, :] = (dot_tn(z, d_b) * inv_root).astype(BF)
        de = dot_nt(d_b, red[lanes, :]) * slope
        column_sum(8 + c, de)
        deb = de.astype(BF)
        put(g_exp, dot_tn(h2, deb), lanes)
        term = dot_nt(deb, exp[:, lanes])
        if c == 0:
            dr1_s[...] = term
        else:
            dr1_s[...] += term
    dh2 = dr1_s[...]
    column_sum(5, dh2 * xhat2)
    column_sum(6, dh2)
    dr1 = d + normalize_backward(dh2 * (1.0 + row(5)), xhat2, inverse2)
    dr1_s[...] = dr1
    column_sum(4, dr1)
    dr1b = dr1.astype(BF)
    put(g_att, dot_tn(o_s[...], dr1b), slice(3 * width, 4 * width))
    do_s[...] = dot_nt(dr1b, att[:, 3 * width :]).astype(BF)
    g_bias[...] = jnp.zeros_like(g_bias)

    def attend_back(w, carry):
        here = pl.ds(pl.multiple_of(w * PADDED, PADDED), PADDED)
        for g in range(groups):
            lanes = slice(g * GROUP, (g + 1) * GROUP)
            prob = p_s[w, g]
            grads = stack_heads(do_s[here, lanes])
            dp = dot_nt(grads, v_s[here, lanes])
            dv = dot_tn(prob.astype(BF), grads)
            ds = prob * (dp - jnp.sum(prob * dp, axis=-1, keepdims=True))
            for h in range(stacked):
                g_bias[g * stacked + h] += ds[h * PADDED : (h + 1) * PADDED]
            dsb = ds.astype(BF)
            dq = pick_heads(dot_nn(dsb, k_s[here, lanes])) * scale
            dk = dot_tn(dsb, stack_heads(q_s[here, lanes]))
            g_vec[2:3, lanes] += jnp.sum(dq, axis=0, keepdims=True)
            g_vec[3:4, lanes] += jnp.sum(dv, axis=0, keepdims=True)
            dqkv_s[here, lanes] = dq.astype(BF)
            dqkv_s[here, width + g * GROUP : width + (g + 1) * GROUP] = dk.astype(BF)
            dqkv_s[here, 2 * width + g * GROUP : 2 * width + (g + 1) * GROUP] = dv.astype(BF)
        return carry

    lax.fori_loop(0, windows, attend_back, 0)

    for c in range(3):
        lanes = slice(c * width, (c + 1) * width)
        put(g_att, dot_tn(h1_s[...], dqkv_s[:, lanes]), lanes)
    dh1 = dot_nt(dqkv_s[...], att[:, : 3 * width])
    column_sum(0, dh1 * xhat1[...])
    column_sum(1, dh1)
    out_dt[...] = dr1_s[...] + normalize_backward(dh1 * (1.0 + row(0)), xhat1[...], inverse1)


def block_on_windows(windows_in, grad_windows, matrices, row_vectors, pos_bias, same, inv_root):
    count, size, width = windows_in.shape
    rows = count * PADDED
    heads = pos_bias.shape[0]

    def padded(blocks):
        return jnp.pad(blocks, ((0, 0), (0, PADDED - size), (0, 0))).reshape(rows, width)

    attention, expand, shrink = matrices
    vm = pltpu.VMEM
    return pl.pallas_call(
        lambda *refs: block_kernel(inv_root, *refs),
        out_shape=(
            jax.ShapeDtypeStruct((rows, width), F32),
            jax.ShapeDtypeStruct((rows, width), F32),
            jax.ShapeDtypeStruct(attention.shape, BF),
            jax.ShapeDtypeStruct(expand.shape, BF),
            jax.ShapeDtypeStruct(shrink.shape, BF),
            jax.ShapeDtypeStruct((16, width), F32),
            jax.ShapeDtypeStruct(pos_bias.shape, F32),
        ),
        in_specs=[VM] * 8,
        out_specs=[VM] * 7,
        scratch_shapes=[
            vm((rows, width), F32), vm((rows, width), BF), vm((rows, width), BF), vm((rows, width), BF),
            vm((rows, width), BF), vm((rows, width), BF), vm((rows, width), BF),
            vm((count, width // GROUP, GROUP * heads // width * PADDED, PADDED), F32),
            vm((rows, 3 * width), BF), vm((rows, width), F32), vm((rows, width), F32),
        ],
        compiler_params=pltpu.CompilerParams(vmem_limit_bytes=48 * 1024 * 1024),
        name="block_on_windows",
    )(padded(windows_in), padded(grad_windows), attention, expand, shrink, row_vectors, pos_bias, same)


def on_device(
    block_input,
    output_grad,
    region_ids,
    relative_index,
    attention_weight,
    expand_weight,
    reduce_weight,
    vectors,
    bias_table,
    attention_mean,
    attention_square,
    expand_mean,
    expand_square,
    reduce_mean,
    reduce_square,
    vectors_mean,
    vectors_square,
    table_mean,
    table_square,
):
    image_count, band_rows, columns, features = block_input.shape
    window_size = WIN * WIN
    shard_count = lax.axis_size("shard")
    band_count = lax.axis_size("band")
    edge_rows = jnp.stack([block_input[:, :SHIFT], output_grad[:, :SHIFT]])
    rows_below = passed_along(edge_rows, "band", -1)
    inner_rows = jnp.stack([block_input[:, SHIFT:], output_grad[:, SHIFT:]])
    shifted = jnp.roll(jnp.concatenate([inner_rows, rows_below], axis=2), -SHIFT, axis=3)
    windows_in = to_windows(shifted[0])
    grad_windows = to_windows(shifted[1])
    pad = PADDED - window_size
    region_windows = jnp.tile(to_windows(region_ids[None]), (image_count, 1))
    region_windows = jnp.pad(region_windows, ((0, 0), (0, pad)), constant_values=-1)
    same_region = (region_windows[:, :, None] == region_windows[:, None, :]).astype(F32)
    table_rows = bias_table.shape[0]
    head_count = bias_table.shape[1]
    padded_index = jnp.pad(relative_index, ((0, pad), (0, pad)), constant_values=-1)
    one_hot = (
        padded_index.reshape(-1)[:, None] == jnp.arange(table_rows, dtype=jnp.int32)[None, :]
    ).astype(jnp.float32)
    pos_bias = jnp.dot(one_hot, bias_table, precision=lax.Precision.HIGHEST).T.reshape(
        head_count, PADDED, PADDED
    )
    feature_rows = attention_weight.shape[0]
    gathered = gather_shards(
        attention_weight.astype(BF),
        expand_weight.astype(BF),
        reduce_weight.astype(BF).reshape(4, feature_rows, features),
        jnp.pad(vectors.astype(BF), ((0, 4), (0, 128 - vectors.shape[1]))),
    )
    matrices = (
        gathered[0].reshape(features, -1),
        gathered[1].reshape(features, -1),
        gathered[2].reshape(-1, features),
    )
    row_vectors_list = (
        jnp.moveaxis(gathered[3][:, :12, : vectors.shape[1]], 0, 1).reshape(12, features).astype(jnp.float32)
    )
    inv_root = 1.0 / math.sqrt(image_count * shard_count * band_rows * band_count * columns)
    output_rows, gradient_token_rows, grad_attention, grad_expand, grad_shrink, grad_vectors, grad_posbias = (
        block_on_windows(
            windows_in, grad_windows, matrices, jnp.pad(row_vectors_list, ((0, 4), (0, 0))), pos_bias,
            same_region, inv_root,
        )
    )
    output_rows = output_rows.reshape(-1, PADDED, features)[:, :window_size]
    gradient_token_rows = gradient_token_rows.reshape(-1, PADDED, features)[:, :window_size]
    grad_vectors = grad_vectors[:12]
    table_local = jnp.dot(
        grad_posbias.reshape(head_count, -1), one_hot, precision=lax.Precision.HIGHEST
    ).T
    vector_terms = grad_vectors.size
    small = jnp.concatenate([grad_vectors.reshape(-1), table_local.reshape(-1)]) * inv_root
    small_rows = -(-small.size // 1024) * 8
    small = jnp.pad(small, (0, small_rows * 128 - small.size)).reshape(small_rows, 128)
    attention_grad, expand_grad, reduce_grad, small_sum = reduce_to_owners(
        grad_attention.reshape(shard_count, feature_rows, -1),
        grad_expand.reshape(shard_count, feature_rows, -1),
        grad_shrink.reshape(shard_count, 4, feature_rows, features),
        small,
    )
    reduce_grad = reduce_grad.reshape(reduce_weight.shape)
    small_sum = small_sum.reshape(-1)
    vectors_grad = lax.dynamic_slice_in_dim(
        small_sum[:vector_terms].reshape(12, features),
        lax.axis_index("shard") * vectors.shape[1],
        vectors.shape[1],
        axis=1,
    )
    table_grad = small_sum[vector_terms : vector_terms + bias_table.size].reshape(bias_table.shape)
    frames = jnp.stack(
        [
            from_windows(
                output_rows.reshape(-1, window_size, features), image_count, band_rows, columns
            ),
            from_windows(
                gradient_token_rows.reshape(-1, window_size, features),
                image_count,
                band_rows,
                columns,
            ),
        ]
    )
    frames = jnp.roll(frames, SHIFT, axis=3)
    rows_above = passed_along(
        frames[:, :, band_rows - SHIFT :].astype(jnp.bfloat16), "band", 1
    ).astype(jnp.float32)
    placed = jnp.concatenate([rows_above, frames[:, :, : band_rows - SHIFT]], axis=2)
    new_attention, new_attention_mean, new_attention_square = adamw(
        attention_weight, attention_grad, attention_mean, attention_square, WEIGHT_DECAY
    )
    new_expand, new_expand_mean, new_expand_square = adamw(
        expand_weight, expand_grad, expand_mean, expand_square, WEIGHT_DECAY
    )
    new_reduce, new_reduce_mean, new_reduce_square = adamw(
        reduce_weight, reduce_grad, reduce_mean, reduce_square, WEIGHT_DECAY
    )
    new_vectors, new_vectors_mean, new_vectors_square = adamw(
        vectors, vectors_grad, vectors_mean, vectors_square, 0.0
    )
    new_table, new_table_mean, new_table_square = adamw(
        bias_table, table_grad, table_mean, table_square, 0.0
    )
    return (
        placed[0],
        placed[1],
        attention_grad,
        expand_grad,
        reduce_grad,
        vectors_grad,
        table_grad,
        new_attention,
        new_expand,
        new_reduce,
        new_vectors,
        new_table,
        new_attention_mean,
        new_attention_square,
        new_expand_mean,
        new_expand_square,
        new_reduce_mean,
        new_reduce_square,
        new_vectors_mean,
        new_vectors_square,
        new_table_mean,
        new_table_square,
    )


def solution(mesh):
    return jax.shard_map(
        on_device,
        mesh=mesh,
        in_specs=(
            P("shard", "band", None, None),
            P("shard", "band", None, None),
            P("band", None),
            P(),
            P("shard", None),
            P("shard", None),
            P("shard", None),
            P(None, "shard"),
            P(),
            P("shard", None),
            P("shard", None),
            P("shard", None),
            P("shard", None),
            P("shard", None),
            P("shard", None),
            P(None, "shard"),
            P(None, "shard"),
            P(),
            P(),
        ),
        out_specs=(
            P("shard", "band", None, None),
            P("shard", "band", None, None),
            P("shard", None),
            P("shard", None),
            P("shard", None),
            P(None, "shard"),
            P(),
            P("shard", None),
            P("shard", None),
            P("shard", None),
            P(None, "shard"),
            P(),
            P("shard", None),
            P("shard", None),
            P("shard", None),
            P("shard", None),
            P("shard", None),
            P("shard", None),
            P(None, "shard"),
            P(None, "shard"),
            P(),
            P(),
        ),
        check_vma=False,
    )
```

```python
import math

import jax
import jax.numpy as jnp
from jax import lax
from jax.experimental import pallas as pl
from jax.experimental.pallas import tpu as pltpu
from jax.sharding import PartitionSpec as P

WIN = 7
SHIFT = 3
STEP = 5


NORM_EPS = 1e-05
LEARN_RATE = 0.02
BETA_ONE = 0.9
BETA_TWO = 0.999
ADAM_EPS = 1e-08
WEIGHT_DECAY = 0.05
MASK_VALUE = -1000000000.0


BF = jnp.bfloat16
F32 = jnp.float32
MESH_ID = pl.DeviceIdType.MESH


def ring_position(index, count):
    column, row = index % 2, index // 2
    return (1 - column) * row + column * (count - 1 - row)


def ring_index(position, count):
    back = position // (count // 2)
    return (1 - back) * (2 * position) + back * (2 * (count - 1 - position) + 1)


def remote(src, dst, send, recv, **where):
    return pltpu.make_async_remote_copy(
        src_ref=src, dst_ref=dst, send_sem=send, recv_sem=recv, device_id=where, device_id_type=MESH_ID
    )


def greet(places):
    barrier = pltpu.get_barrier_semaphore()
    for where in places:
        pl.semaphore_signal(barrier, inc=1, device_id=where, device_id_type=MESH_ID)
    pl.semaphore_wait(barrier, len(places))


def gather_kernel(
    count, att, exp, red, vec, out_att, out_exp, out_red, out_vec,
    ring_send, ring_recv, pair_send, pair_recv, vec_send, vec_recv, own_sem,
):
    shard = lax.axis_index("shard")
    band = lax.axis_index("band")
    core = band % 2
    partner = band + 1 - 2 * core
    pos = ring_position(shard, count)
    to_right = ring_index((pos + 1) % count, count)
    to_left = ring_index((pos + count - 1) % count, count)
    peers = [(shard + j) % count for j in range(1, count)]
    greet([{"shard": peer} for peer in peers] + [{"band": partner}])

    def parts(block, quarter):
        lanes = pl.ds(pl.multiple_of(quarter * 512, 512), 512)
        return (
            out_att.at[block, :, lanes],
            out_exp.at[block, :, lanes],
            out_red.at[block, quarter],
        )

    def own_parts(quarter):
        lanes = pl.ds(pl.multiple_of(quarter * 512, 512), 512)
        return (att.at[:, lanes], exp.at[:, lanes], red.at[quarter])

    sends = []

    def send_ring(way, step):
        quarter = 2 * core + way
        block = ring_index((pos - step + count) % count if way == 0 else (pos + step) % count, count)
        target = to_right if way == 0 else to_left
        sources = own_parts(quarter) if step == 0 else parts(block, quarter)
        for k, (source, place) in enumerate(zip(sources, parts(block, quarter))):
            copy = remote(source, place, ring_send.at[way, step, k], ring_recv.at[way, step, k], shard=target)
            copy.start()
            sends.append(copy)

    for way in range(2):
        send_ring(way, 0)
    own = [
        pltpu.make_async_copy(source, place, own_sem.at[k])
        for k, (source, place) in enumerate(
            ((att, out_att.at[shard]), (exp, out_exp.at[shard]), (red, out_red.at[shard]), (vec, out_vec.at[shard]))
        )
    ]
    for copy in own:
        copy.start()
    for peer, j in zip(peers, range(count - 1)):
        copy = remote(vec, out_vec.at[shard], vec_send.at[j], vec_recv.at[j], shard=peer)
        copy.start()
        sends.append(copy)
    for step in range(count - 1):
        for way in range(2):
            quarter = 2 * core + way
            block = ring_index(
                (pos - step - 1 + count) % count if way == 0 else (pos + step + 1) % count, count
            )
            places = parts(block, quarter)
            for k, place in enumerate(places):
                remote(
                    place, place, ring_send.at[way, step, k], ring_recv.at[way, step, k], shard=to_right
                ).wait_recv()
            if step < count - 2:
                send_ring(way, step + 1)
            for k, place in enumerate(places):
                copy = remote(place, place, pair_send.at[way, step, k], pair_recv.at[way, step, k], band=partner)
                copy.start()
                sends.append(copy)
    for step in range(count - 1):
        for way in range(2):
            quarter = 2 * (1 - core) + way
            block = ring_index(
                (pos - step - 1 + count) % count if way == 0 else (pos + step + 1) % count, count
            )
            for k, place in enumerate(parts(block, quarter)):
                remote(
                    place, place, pair_send.at[way, step, k], pair_recv.at[way, step, k], band=partner
                ).wait_recv()
    for j in range(count - 1):
        source = (shard + count - 1 - j) % count
        remote(vec, out_vec.at[source], vec_send.at[j], vec_recv.at[j], shard=source).wait_recv()
    for copy in sends:
        copy.wait_send()
    for copy in own:
        copy.wait()


VM = pl.BlockSpec(memory_space=pltpu.VMEM)


def gather_shards(att, exp, red, vec):
    count = lax.axis_size("shard")
    rows = att.shape[0]
    dma = pltpu.SemaphoreType.DMA
    return pl.pallas_call(
        lambda *refs: gather_kernel(count, *refs),
        out_shape=(
            jax.ShapeDtypeStruct((count, rows, att.shape[1]), BF),
            jax.ShapeDtypeStruct((count, rows, exp.shape[1]), BF),
            jax.ShapeDtypeStruct((count,) + red.shape, BF),
            jax.ShapeDtypeStruct((count,) + vec.shape, BF),
        ),
        in_specs=[VM] * 4,
        out_specs=[VM] * 4,
        scratch_shapes=[
            dma((2, count - 1, 3)), dma((2, count - 1, 3)), dma((2, count - 1, 3)), dma((2, count - 1, 3)),
            dma((count - 1,)), dma((count - 1,)), dma((4,)),
        ],
        compiler_params=pltpu.CompilerParams(
            collective_id=0, has_side_effects=True, vmem_limit_bytes=12 * 1024 * 1024
        ),
        name="gather_shards",
    )(att, exp, red, vec)


def reduce_kernel(
    count, bands, att, exp, red, small, out_att, out_exp, out_red, out_small,
    paired, sent, got, done, others, mixed, small_band, small_shard,
    pair_send, pair_recv, ring_send, ring_recv, far_send, far_recv, mix_send, mix_recv,
    sb_send, sb_recv, ss_send, ss_recv,
):
    shard = lax.axis_index("shard")
    band = lax.axis_index("band")
    core = band % 2
    partner = band + 1 - 2 * core
    pos = ring_position(shard, count)
    to_right = ring_index((pos + 1) % count, count)
    to_left = ring_index((pos + count - 1) % count, count)
    shard_peers = [(shard + j) % count for j in range(1, count)]
    band_peers = [(band + j) % bands for j in range(1, bands)]
    rows = att.shape[1]
    greet([{"shard": peer} for peer in shard_peers] + [{"band": peer} for peer in band_peers])

    def block_of(way, step):
        if way == 0:
            return ring_index((pos - 1 - step + 2 * count) % count, count)
        return ring_index((pos + 1 + step) % count, count)

    def own_parts(block, quarter):
        lanes = pl.ds(pl.multiple_of(quarter * 512, 512), 512)
        return (att.at[block, :, lanes], exp.at[block, :, lanes], red.at[block, quarter])

    waits = []

    def pair_copy(way, step, k):
        block = block_of(way, step)
        source = own_parts(block, 2 * (1 - core) + way)[k]
        return remote(
            source, paired.at[way, step, k], pair_send.at[way, step, k], pair_recv.at[way, step, k], band=partner
        )

    for step in range(count):
        for way in range(2):
            for k in range(3):
                copy = pair_copy(way, step, k)
                copy.start()
                waits.append(copy)
        if step == 0:
            small_band[band] = small[...]
            for j, peer in enumerate(band_peers):
                copy = remote(small, small_band.at[band], sb_send.at[j], sb_recv.at[j], band=peer)
                copy.start()
                waits.append(copy)

    for step in range(count):
        for way in range(2):
            block = block_of(way, step)
            quarter = 2 * core + way
            if step > 0:
                remote(
                    sent.at[way, step - 1], got.at[way, step - 1],
                    ring_send.at[way, step - 1], ring_recv.at[way, step - 1], shard=to_right,
                ).wait_recv()
            lanes = pl.ds(pl.multiple_of(quarter * 512, 512), 512)
            for k in range(3):
                pair_copy(way, step, k).wait_recv()
                mine = (
                    att[block, :, lanes] if k == 0 else exp[block, :, lanes] if k == 1 else red[block, quarter]
                )
                total = mine.astype(F32) + paired[way, step, k].astype(F32)
                if step > 0:
                    total = total + got[way, step - 1, k].astype(F32)
                if step < count - 1:
                    sent[way, step, k] = total.astype(BF)
                else:
                    done[way, k] = total.astype(BF)
            if step < count - 1:
                copy = remote(
                    sent.at[way, step], got.at[way, step], ring_send.at[way, step], ring_recv.at[way, step],
                    shard=to_right if way == 0 else to_left,
                )
            else:
                for j in range(1, bands // 2):
                    copy = remote(
                        done.at[way], others.at[j - 1, way], far_send.at[j - 1, way], far_recv.at[j - 1, way],
                        band=(band + 2 * j) % bands,
                    )
                    copy.start()
                    waits.append(copy)
                continue
            copy.start()
            waits.append(copy)
        if step == 0:
            for j in range(bands - 1):
                source = (band + bands - 1 - j) % bands
                remote(small, small_band.at[source], sb_send.at[j], sb_recv.at[j], band=source).wait_recv()
            total = small_band[0]
            for j in range(1, bands):
                total = total + small_band[j]
            small_shard[shard] = total
            for j, peer in enumerate(shard_peers):
                copy = remote(
                    small_shard.at[shard], small_shard.at[shard], ss_send.at[j], ss_recv.at[j], shard=peer
                )
                copy.start()
                waits.append(copy)

    for way in range(2):
        for j in range(1, bands // 2):
            remote(
                done.at[way], others.at[j - 1, way], far_send.at[j - 1, way], far_recv.at[j - 1, way], band=partner
            ).wait_recv()
        total = done[way].astype(F32)
        for j in range(1, bands // 2):
            total = total + others[j - 1, way].astype(F32)
        mixed[core, way] = total.astype(BF)
        copy = remote(
            mixed.at[core, way], mixed.at[core, way], mix_send.at[way], mix_recv.at[way], band=partner
        )
        copy.start()
        waits.append(copy)
    for j in range(count - 1):
        source = (shard + count - 1 - j) % count
        remote(small, small_shard.at[source], ss_send.at[j], ss_recv.at[j], shard=source).wait_recv()
    total = small_shard[0]
    for j in range(1, count):
        total = total + small_shard[j]
    out_small[...] = total
    for way in range(2):
        remote(
            mixed.at[core, way], mixed.at[1 - core, way], mix_send.at[way], mix_recv.at[way], band=partner
        ).wait_recv()
    for quarter in range(4):
        out_att[:, quarter * 512 : quarter * 512 + 512] = mixed[quarter // 2, quarter % 2, 0].astype(F32)
        out_exp[:, quarter * 512 : quarter * 512 + 512] = mixed[quarter // 2, quarter % 2, 1].astype(F32)
        out_red[quarter] = mixed[quarter // 2, quarter % 2, 2].astype(F32)
    for copy in waits:
        copy.wait_send()


def reduce_to_owners(att, exp, red, small):
    count = lax.axis_size("shard")
    bands = lax.axis_size("band")
    rows = att.shape[1]
    dma = pltpu.SemaphoreType.DMA
    far = max(bands // 2 - 1, 1)
    return pl.pallas_call(
        lambda *refs: reduce_kernel(count, bands, *refs),
        out_shape=(
            jax.ShapeDtypeStruct(att.shape[1:], F32),
            jax.ShapeDtypeStruct(exp.shape[1:], F32),
            jax.ShapeDtypeStruct(red.shape[1:], F32),
            jax.ShapeDtypeStruct(small.shape, F32),
        ),
        in_specs=[VM] * 4,
        out_specs=[VM] * 4,
        scratch_shapes=[
            pltpu.VMEM((2, count, 3, rows, 512), BF),
            pltpu.VMEM((2, count - 1, 3, rows, 512), BF),
            pltpu.VMEM((2, count - 1, 3, rows, 512), BF),
            pltpu.VMEM((2, 3, rows, 512), BF),
            pltpu.VMEM((far, 2, 3, rows, 512), BF),
            pltpu.VMEM((2, 2, 3, rows, 512), BF),
            pltpu.VMEM((bands,) + small.shape, F32),
            pltpu.VMEM((count,) + small.shape, F32),
            dma((2, count, 3)), dma((2, count, 3)), dma((2, count - 1)), dma((2, count - 1)),
            dma((far, 2)), dma((far, 2)), dma((2,)), dma((2,)),
            dma((bands - 1,)), dma((bands - 1,)), dma((count - 1,)), dma((count - 1,)),
        ],
        compiler_params=pltpu.CompilerParams(
            collective_id=1, has_side_effects=True, vmem_limit_bytes=24 * 1024 * 1024
        ),
        name="reduce_to_owners",
    )(att, exp, red, small)


def passed_along(block, axis, distance):
    devices = range(lax.axis_size(axis))
    route = [((i - distance) % len(devices), i) for i in devices]
    return lax.ppermute(block, axis, route)


def to_windows(frame):
    image_count, rows_total, cols_total = (frame.shape[0], frame.shape[1], frame.shape[2])
    trailing = frame.shape[3:]
    blocks = frame.reshape((image_count, rows_total // WIN, WIN, cols_total // WIN, WIN) + trailing)
    blocks = jnp.moveaxis(blocks, 3, 2)
    return blocks.reshape(
        (image_count * (rows_total // WIN) * (cols_total // WIN), WIN * WIN) + trailing
    )


def from_windows(blocks, image_count, rows_total, cols_total):
    trailing = blocks.shape[2:]
    frame = blocks.reshape((image_count, rows_total // WIN, cols_total // WIN, WIN, WIN) + trailing)
    frame = jnp.moveaxis(frame, 3, 2)
    return frame.reshape((image_count, rows_total, cols_total) + trailing)


def layer_normalize(values):
    center = jnp.mean(values, axis=-1, keepdims=True)
    centered = values - center
    variance = jnp.mean(centered * centered, axis=-1, keepdims=True)
    inverse_deviation = lax.rsqrt(variance + NORM_EPS)
    return (centered * inverse_deviation, inverse_deviation)


def normalize_backward(gradient_standardized, standardized_input, inverse_deviation):
    return inverse_deviation * (
        gradient_standardized
        - jnp.mean(gradient_standardized, axis=-1, keepdims=True)
        - standardized_input
        * jnp.mean(gradient_standardized * standardized_input, axis=-1, keepdims=True)
    )


def gelu_parts(hidden_pre):
    normal_cdf = 0.5 * (1.0 + lax.erf(hidden_pre * (1.0 / math.sqrt(2.0))))
    density = jnp.exp(-0.5 * hidden_pre * hidden_pre) * (1.0 / math.sqrt(2.0 * math.pi))
    return (hidden_pre * normal_cdf, normal_cdf + hidden_pre * density)


def adamw(weight, grad, first, second, decay):
    first_new = BETA_ONE * first + (1.0 - BETA_ONE) * grad
    second_new = BETA_TWO * second + (1.0 - BETA_TWO) * grad * grad
    corr_one = 1.0 - BETA_ONE**STEP
    corr_two = 1.0 - BETA_TWO**STEP
    step_dir = first_new / corr_one / (jnp.sqrt(second_new / corr_two) + ADAM_EPS)
    return (weight - LEARN_RATE * (step_dir + decay * weight), first_new, second_new)


PADDED = 64
GROUP = 128


def dot_nn(a, b):
    return jnp.dot(a, b, preferred_element_type=F32)


def dot_tn(a, b):
    return lax.dot_general(a, b, (((0,), (0,)), ((), ())), preferred_element_type=F32)


def dot_nt(a, b):
    return lax.dot_general(a, b, (((1,), (1,)), ((), ())), preferred_element_type=F32)


def block_kernel(
    inv_root, x_ref, d_ref, att, exp, red, vec, bias, same,
    out_y, out_dt, g_att, g_exp, g_red, g_vec, g_bias,
    xhat1, q_s, k_s, v_s, h1_s, o_s, do_s, p_s, dqkv_s, r1_s, dr1_s,
):
    rows, width = x_ref.shape
    windows = rows // PADDED
    heads = bias.shape[0]
    head_width = width // heads
    stacked = GROUP // head_width
    groups = width // GROUP
    scale = 1.0 / math.sqrt(head_width)

    def row(k):
        return vec[k : k + 1, :]

    def normed(values):
        centered = values - jnp.mean(values, axis=-1, keepdims=True)
        inverse = lax.rsqrt(jnp.mean(centered * centered, axis=-1, keepdims=True) + NORM_EPS)
        return centered * inverse, inverse

    def put(ref, value, lanes=None):
        value = (value * inv_root).astype(BF)
        if lanes is None:
            ref[...] = value
        else:
            ref[:, lanes] = value

    def column_sum(k, value):
        g_vec[k : k + 1, :] = jnp.sum(value, axis=0, keepdims=True)

    lane = lax.broadcasted_iota(jnp.int32, (1, GROUP), 1) // head_width

    def stack_heads(block):
        zero = jnp.zeros_like(block)
        return jnp.concatenate([jnp.where(lane == h, block, zero) for h in range(stacked)], axis=0)

    def pick_heads(block):
        total = jnp.where(lane == 0, block[:PADDED], 0.0)
        for h in range(1, stacked):
            total = jnp.where(lane == h, block[h * PADDED : (h + 1) * PADDED], total)
        return total

    g_vec[...] = jnp.zeros_like(g_vec)
    standard, inverse1 = normed(x_ref[...].astype(F32))
    xhat1[...] = standard
    h1_s[...] = (standard * (1.0 + row(0)) + row(1)).astype(BF)
    q_s[...] = ((dot_nn(h1_s[...], att[:, :width]) + row(2)) * scale).astype(BF)
    k_s[...] = dot_nn(h1_s[...], att[:, width : 2 * width]).astype(BF)
    v_s[...] = (dot_nn(h1_s[...], att[:, 2 * width : 3 * width]) + row(3)).astype(BF)

    def attend(w, carry):
        here = pl.ds(pl.multiple_of(w * PADDED, PADDED), PADDED)
        allowed = jnp.concatenate([same[w]] * stacked, axis=0) > 0.5
        for g in range(groups):
            lanes = slice(g * GROUP, (g + 1) * GROUP)
            scores = dot_nt(stack_heads(q_s[here, lanes]), k_s[here, lanes])
            shift = jnp.concatenate([bias[g * stacked + h] for h in range(stacked)], axis=0)
            scores = jnp.where(allowed, scores + shift, MASK_VALUE)
            powers = jnp.exp(scores - jnp.max(scores, axis=-1, keepdims=True))
            prob = powers / jnp.sum(powers, axis=-1, keepdims=True)
            p_s[w, g] = prob
            o_s[here, lanes] = pick_heads(dot_nn(prob.astype(BF), v_s[here, lanes])).astype(BF)
        return carry

    lax.fori_loop(0, windows, attend, 0)

    r1_s[...] = x_ref[...].astype(F32) + dot_nn(o_s[...], att[:, 3 * width :]) + row(4)
    xhat2, inverse2 = normed(r1_s[...])
    h2 = (xhat2 * (1.0 + row(5)) + row(6)).astype(BF)
    d_b = d_ref[...]
    d = d_b.astype(F32)
    column_sum(7, d)
    out_y[...] = r1_s[...] + row(7)
    chunks = exp.shape[1] // width
    for c in range(chunks):
        lanes = slice(c * width, (c + 1) * width)
        pre = dot_nn(h2, exp[:, lanes]) + row(8 + c)
        activated, slope = gelu_parts(pre)
        z = activated.astype(BF)
        out_y[...] += dot_nn(z, red[lanes, :])
        g_red[lanes, :] = (dot_tn(z, d_b) * inv_root).astype(BF)
        de = dot_nt(d_b, red[lanes, :]) * slope
        column_sum(8 + c, de)
        deb = de.astype(BF)
        put(g_exp, dot_tn(h2, deb), lanes)
        term = dot_nt(deb, exp[:, lanes])
        if c == 0:
            dr1_s[...] = term
        else:
            dr1_s[...] += term
    dh2 = dr1_s[...]
    column_sum(5, dh2 * xhat2)
    column_sum(6, dh2)
    dr1 = d + normalize_backward(dh2 * (1.0 + row(5)), xhat2, inverse2)
    dr1_s[...] = dr1
    column_sum(4, dr1)
    dr1b = dr1.astype(BF)
    put(g_att, dot_tn(o_s[...], dr1b), slice(3 * width, 4 * width))
    do_s[...] = dot_nt(dr1b, att[:, 3 * width :]).astype(BF)
    g_bias[...] = jnp.zeros_like(g_bias)

    def attend_back(w, carry):
        here = pl.ds(pl.multiple_of(w * PADDED, PADDED), PADDED)
        for g in range(groups):
            lanes = slice(g * GROUP, (g + 1) * GROUP)
            prob = p_s[w, g]
            grads = stack_heads(do_s[here, lanes])
            dp = dot_nt(grads, v_s[here, lanes])
            dv = dot_tn(prob.astype(BF), grads)
            ds = prob * (dp - jnp.sum(prob * dp, axis=-1, keepdims=True))
            for h in range(stacked):
                g_bias[g * stacked + h] += ds[h * PADDED : (h + 1) * PADDED]
            dsb = ds.astype(BF)
            dq = pick_heads(dot_nn(dsb, k_s[here, lanes])) * scale
            dk = dot_tn(dsb, stack_heads(q_s[here, lanes]))
            g_vec[2:3, lanes] += jnp.sum(dq, axis=0, keepdims=True)
            g_vec[3:4, lanes] += jnp.sum(dv, axis=0, keepdims=True)
            dqkv_s[here, lanes] = dq.astype(BF)
            dqkv_s[here, width + g * GROUP : width + (g + 1) * GROUP] = dk.astype(BF)
            dqkv_s[here, 2 * width + g * GROUP : 2 * width + (g + 1) * GROUP] = dv.astype(BF)
        return carry

    lax.fori_loop(0, windows, attend_back, 0)

    for c in range(3):
        lanes = slice(c * width, (c + 1) * width)
        put(g_att, dot_tn(h1_s[...], dqkv_s[:, lanes]), lanes)
    dh1 = dot_nt(dqkv_s[...], att[:, : 3 * width])
    column_sum(0, dh1 * xhat1[...])
    column_sum(1, dh1)
    out_dt[...] = dr1_s[...] + normalize_backward(dh1 * (1.0 + row(0)), xhat1[...], inverse1)


def block_on_windows(windows_in, grad_windows, matrices, row_vectors, pos_bias, same, inv_root):
    count, size, width = windows_in.shape
    rows = count * PADDED
    heads = pos_bias.shape[0]

    def padded(blocks):
        return jnp.pad(blocks, ((0, 0), (0, PADDED - size), (0, 0))).reshape(rows, width)

    attention, expand, shrink = matrices
    vm = pltpu.VMEM
    return pl.pallas_call(
        lambda *refs: block_kernel(inv_root, *refs),
        out_shape=(
            jax.ShapeDtypeStruct((rows, width), F32),
            jax.ShapeDtypeStruct((rows, width), F32),
            jax.ShapeDtypeStruct(attention.shape, BF),
            jax.ShapeDtypeStruct(expand.shape, BF),
            jax.ShapeDtypeStruct(shrink.shape, BF),
            jax.ShapeDtypeStruct((16, width), F32),
            jax.ShapeDtypeStruct(pos_bias.shape, F32),
        ),
        in_specs=[VM] * 8,
        out_specs=[VM] * 7,
        scratch_shapes=[
            vm((rows, width), F32), vm((rows, width), BF), vm((rows, width), BF), vm((rows, width), BF),
            vm((rows, width), BF), vm((rows, width), BF), vm((rows, width), BF),
            vm((count, width // GROUP, GROUP * heads // width * PADDED, PADDED), F32),
            vm((rows, 3 * width), BF), vm((rows, width), F32), vm((rows, width), F32),
        ],
        compiler_params=pltpu.CompilerParams(vmem_limit_bytes=28 * 1024 * 1024),
        name="block_on_windows",
    )(padded(windows_in), padded(grad_windows), attention, expand, shrink, row_vectors, pos_bias, same)


def on_device(
    block_input,
    output_grad,
    region_ids,
    relative_index,
    attention_weight,
    expand_weight,
    reduce_weight,
    vectors,
    bias_table,
    attention_mean,
    attention_square,
    expand_mean,
    expand_square,
    reduce_mean,
    reduce_square,
    vectors_mean,
    vectors_square,
    table_mean,
    table_square,
):
    image_count, band_rows, columns, features = block_input.shape
    window_size = WIN * WIN
    shard_count = lax.axis_size("shard")
    band_count = lax.axis_size("band")
    edge_rows = jnp.stack([block_input[:, :SHIFT], output_grad[:, :SHIFT]])
    rows_below = passed_along(edge_rows, "band", -1)
    inner_rows = jnp.stack([block_input[:, SHIFT:], output_grad[:, SHIFT:]])
    shifted = jnp.roll(jnp.concatenate([inner_rows, rows_below], axis=2), -SHIFT, axis=3)
    windows_in = to_windows(shifted[0])
    grad_windows = to_windows(shifted[1])
    pad = PADDED - window_size
    region_windows = jnp.tile(to_windows(region_ids[None]), (image_count, 1))
    region_windows = jnp.pad(region_windows, ((0, 0), (0, pad)), constant_values=-1)
    same_region = (region_windows[:, :, None] == region_windows[:, None, :]).astype(F32)
    table_rows = bias_table.shape[0]
    head_count = bias_table.shape[1]
    padded_index = jnp.pad(relative_index, ((0, pad), (0, pad)), constant_values=-1)
    one_hot = (
        padded_index.reshape(-1)[:, None] == jnp.arange(table_rows, dtype=jnp.int32)[None, :]
    ).astype(jnp.float32)
    pos_bias = jnp.dot(one_hot, bias_table, precision=lax.Precision.HIGHEST).T.reshape(
        head_count, PADDED, PADDED
    )
    feature_rows = attention_weight.shape[0]
    gathered = gather_shards(
        attention_weight.astype(BF),
        expand_weight.astype(BF),
        reduce_weight.astype(BF).reshape(4, feature_rows, features),
        jnp.pad(vectors.astype(BF), ((0, 4), (0, 128 - vectors.shape[1]))),
    )
    matrices = (
        gathered[0].reshape(features, -1),
        gathered[1].reshape(features, -1),
        gathered[2].reshape(-1, features),
    )
    row_vectors_list = (
        jnp.moveaxis(gathered[3][:, :12, : vectors.shape[1]], 0, 1).reshape(12, features).astype(jnp.float32)
    )
    inv_root = 1.0 / math.sqrt(image_count * shard_count * band_rows * band_count * columns)
    output_rows, gradient_token_rows, grad_attention, grad_expand, grad_shrink, grad_vectors, grad_posbias = (
        block_on_windows(
            windows_in, grad_windows, matrices, jnp.pad(row_vectors_list, ((0, 4), (0, 0))), pos_bias,
            same_region, inv_root,
        )
    )
    output_rows = output_rows.reshape(-1, PADDED, features)[:, :window_size]
    gradient_token_rows = gradient_token_rows.reshape(-1, PADDED, features)[:, :window_size]
    grad_vectors = grad_vectors[:12]
    table_local = jnp.dot(
        grad_posbias.reshape(head_count, -1), one_hot, precision=lax.Precision.HIGHEST
    ).T
    vector_terms = grad_vectors.size
    small = jnp.concatenate([grad_vectors.reshape(-1), table_local.reshape(-1)]) * inv_root
    small_rows = -(-small.size // 1024) * 8
    small = jnp.pad(small, (0, small_rows * 128 - small.size)).reshape(small_rows, 128)
    attention_grad, expand_grad, reduce_grad, small_sum = reduce_to_owners(
        grad_attention.reshape(shard_count, feature_rows, -1),
        grad_expand.reshape(shard_count, feature_rows, -1),
        grad_shrink.reshape(shard_count, 4, feature_rows, features),
        small,
    )
    reduce_grad = reduce_grad.reshape(reduce_weight.shape)
    small_sum = small_sum.reshape(-1)
    vectors_grad = lax.dynamic_slice_in_dim(
        small_sum[:vector_terms].reshape(12, features),
        lax.axis_index("shard") * vectors.shape[1],
        vectors.shape[1],
        axis=1,
    )
    table_grad = small_sum[vector_terms : vector_terms + bias_table.size].reshape(bias_table.shape)
    frames = jnp.stack(
        [
            from_windows(
                output_rows.reshape(-1, window_size, features), image_count, band_rows, columns
            ),
            from_windows(
                gradient_token_rows.reshape(-1, window_size, features),
                image_count,
                band_rows,
                columns,
            ),
        ]
    )
    frames = jnp.roll(frames, SHIFT, axis=3)
    rows_above = passed_along(
        frames[:, :, band_rows - SHIFT :].astype(jnp.bfloat16), "band", 1
    ).astype(jnp.float32)
    placed = jnp.concatenate([rows_above, frames[:, :, : band_rows - SHIFT]], axis=2)
    new_attention, new_attention_mean, new_attention_square = adamw(
        attention_weight, attention_grad, attention_mean, attention_square, WEIGHT_DECAY
    )
    new_expand, new_expand_mean, new_expand_square = adamw(
        expand_weight, expand_grad, expand_mean, expand_square, WEIGHT_DECAY
    )
    new_reduce, new_reduce_mean, new_reduce_square = adamw(
        reduce_weight, reduce_grad, reduce_mean, reduce_square, WEIGHT_DECAY
    )
    new_vectors, new_vectors_mean, new_vectors_square = adamw(
        vectors, vectors_grad, vectors_mean, vectors_square, 0.0
    )
    new_table, new_table_mean, new_table_square = adamw(
        bias_table, table_grad, table_mean, table_square, 0.0
    )
    return (
        placed[0],
        placed[1],
        attention_grad,
        expand_grad,
        reduce_grad,
        vectors_grad,
        table_grad,
        new_attention,
        new_expand,
        new_reduce,
        new_vectors,
        new_table,
        new_attention_mean,
        new_attention_square,
        new_expand_mean,
        new_expand_square,
        new_reduce_mean,
        new_reduce_square,
        new_vectors_mean,
        new_vectors_square,
        new_table_mean,
        new_table_square,
    )


def solution(mesh):
    return jax.shard_map(
        on_device,
        mesh=mesh,
        in_specs=(
            P("shard", "band", None, None),
            P("shard", "band", None, None),
            P("band", None),
            P(),
            P("shard", None),
            P("shard", None),
            P("shard", None),
            P(None, "shard"),
            P(),
            P("shard", None),
            P("shard", None),
            P("shard", None),
            P("shard", None),
            P("shard", None),
            P("shard", None),
            P(None, "shard"),
            P(None, "shard"),
            P(),
            P(),
        ),
        out_specs=(
            P("shard", "band", None, None),
            P("shard", "band", None, None),
            P("shard", None),
            P("shard", None),
            P("shard", None),
            P(None, "shard"),
            P(),
            P("shard", None),
            P("shard", None),
            P("shard", None),
            P(None, "shard"),
            P(),
            P("shard", None),
            P("shard", None),
            P("shard", None),
            P("shard", None),
            P("shard", None),
            P("shard", None),
            P(None, "shard"),
            P(None, "shard"),
            P(),
            P(),
        ),
        check_vma=False,
    )
```
